32 devices in a mesh: hour: 2 (over y), stn: 4 (over x, core), tchunk: 4 (over z).
Axes of the slice: x: 2, y: 2, z: 4, core: 2. Of those that a mesh axis runs over, the one named last changes fastest.
Arguments:
- raw_data: float32 [576, 32768], P('stn', ('hour', 'tchunk')), parts along dimension 1, may hold values from -500 to 500, as said below
- station_group: int32 [576], P('stn'), may hold values from 0 to 15
- partner_blocks: int32 [4, 3], P('stn'), may hold values from -1 to 3, as said below
Outputs:
- cross_spectra: float32 [8, 3, 512, 512], P(('hour', 'stn'), None, 'tchunk'), parts along dimension 0
The draws below stay inside these ranges and needn't reach their ends.
There are 2 independent parts, one for each index of `hour`. The reference program is written for one: setup_inputs(seed, part) draws one part's arguments, and reference() takes and returns one part's arrays. A program takes and returns all parts, laid end to end along the dimension named above; an argument that names none is the same for every part. Nothing has to cross between parts.
Inputs may be any that keep to these rules, and one draw needn't show every extreme that they name: `raw_data`: recorded ground motion. `partner_blocks`: row b holds distinct blocks other than b in its first entries and -1 in the rest; every row has at least one partner and some row has 3.
All inputs are finite; a program needn't handle non-finite values.
Results may differ from the reference program's by a relative error of at most 0.0079.
Values may be sent and summed in bfloat16 or wider, within the bound.
A program may use at most 128 MiB of HBM per device.

```python
import math
import jax
import jax.numpy as jnp
from jax import lax

STN_DEV = 144
SEGLEN = 4096
HOP = 2048
NBIN = 512
RB = 128
RAMH = 10
SMOOTH = 8
SUB = 16
MAXP = 3
NBLK = 4
STATIONS = 576
SAMPLES = 16384
NSEG = 7


def draw_raw_data(key, part):
    total_blocks = SAMPLES // RB
    station_scale = jnp.exp(jax.random.uniform(jax.random.fold_in(key, 101), (STATIONS, 1, 1), minval=math.log(0.1), maxval=math.log(10.0)))
    envelope = jnp.exp(jax.random.uniform(jax.random.fold_in(key, 102), (STATIONS, total_blocks, 1), minval=0.0, maxval=math.log(10.0)))
    base_motion = jnp.clip(jax.random.normal(jax.random.fold_in(key, 103), (STATIONS, total_blocks, RB)), -4.0, 4.0)
    values = station_scale * envelope * base_motion
    return values.reshape(STATIONS, SAMPLES).astype(jnp.float32)


def draw_partner_blocks(key, part):
    block_rows = jnp.arange(NBLK, dtype=jnp.int32)

    def one_row(block_row):
        shuffle = jax.random.permutation(jax.random.fold_in(key, block_row), NBLK - 1).astype(jnp.int32)
        return (block_row + 1 + shuffle[:MAXP]) % NBLK
    chosen = jax.vmap(one_row)(block_rows)
    partner_count = jax.random.randint(jax.random.fold_in(key, 7001), (NBLK,), 1, MAXP + 1)
    full_row = jax.random.randint(jax.random.fold_in(key, 7002), (), 0, NBLK)
    partner_count = jnp.where(block_rows == full_row, MAXP, partner_count)
    slot_index = jnp.arange(MAXP, dtype=jnp.int32)
    return jnp.where(slot_index[None, :] < partner_count[:, None], chosen, -1).astype(jnp.int32)


def touch_ends(values, stream_key, least, high):
    index_at = [jax.random.randint(jax.random.fold_in(stream_key, axis), (), 0, length) for axis, length in enumerate(values.shape)]
    widest = values.shape.index(max(values.shape))
    neighbour = index_at[:widest] + [(index_at[widest] + 1) % values.shape[widest]] + index_at[widest + 1:]
    return values.at[tuple(index_at)].set(least).at[tuple(neighbour)].set(high)


def setup_inputs(seed: int = 0, part: int = 0) -> dict:
    streams_of = jax.random.split(jax.random.key(seed), 4)
    part_keys = jax.random.split(jax.random.fold_in(streams_of[3], part), 4)
    return {
        "raw_data": draw_raw_data(jax.random.fold_in(jax.random.fold_in(streams_of[3], part), 71), part),
        "station_group": touch_ends(jax.random.randint(streams_of[1], (STATIONS,), 0, SUB), jax.random.fold_in(streams_of[1], 1), 0, SUB - 1).astype(jnp.int32),
        "partner_blocks": draw_partner_blocks(jax.random.fold_in(streams_of[3], 71), part),
    }


EPS_MEAN = 1e-06
LEVEL = 0.05

def dft_table():
    sample = jnp.arange(SEGLEN, dtype=jnp.int32)
    frequency = jnp.arange(1, NBIN + 1, dtype=jnp.int32)
    phases = sample[:, None] * frequency[None, :] % SEGLEN
    angles = phases.astype(jnp.float32) * (2.0 * math.pi / SEGLEN)
    taper_window = 0.5 - 0.5 * jnp.cos(sample.astype(jnp.float32) * (2.0 * math.pi / SEGLEN))
    matrix = jnp.concatenate([taper_window[:, None] * jnp.cos(angles), -taper_window[:, None] * jnp.sin(angles)], axis=1)
    return matrix.astype(jnp.bfloat16)

def smooth_table():
    bin_index = jnp.arange(NBIN, dtype=jnp.int32)
    nearby = (jnp.abs(bin_index[:, None] - bin_index[None, :]) <= SMOOTH).astype(jnp.float32)
    return nearby / lax.optimization_barrier(jnp.sum(nearby, axis=0, keepdims=True))

def whiten(spectra, smoother):
    real_part = spectra[:, :NBIN]
    imag_part = spectra[:, NBIN:]
    powers = real_part * real_part + imag_part * imag_part
    smooth = jnp.dot(powers, smoother, precision=lax.Precision.HIGHEST)
    floor_level = lax.optimization_barrier(jnp.mean(powers, axis=1, keepdims=True)) + 1e-06
    divisor = jnp.sqrt(smooth + LEVEL * floor_level)
    return jnp.concatenate([real_part / divisor, imag_part / divisor], axis=1).astype(jnp.bfloat16)

def cross_terms(mine, others):
    mine = mine.astype(jnp.float32)
    others = others.astype(jnp.float32)
    real_part = mine[:, :, 0]
    imag_part = mine[:, :, 1]
    left_side = jnp.stack([jnp.stack([real_part, imag_part], 2), jnp.stack([imag_part, -real_part], 2)], 0)
    product = jnp.einsum('oqsck,mrsck->mkoqr', left_side, others, precision=lax.Precision.HIGHEST)
    return product.reshape(product.shape[0], product.shape[1], -1)

def reference(raw_data, station_group, partner_blocks):
    total_blocks = SAMPLES // RB
    pieces = raw_data.reshape(STATIONS, total_blocks, RB)
    block_sums = lax.optimization_barrier(jnp.sum(jnp.abs(pieces), axis=2))
    padded = jnp.pad(block_sums, ((0, 0), (RAMH, RAMH)))
    window = padded[:, 0:total_blocks]
    for offset in range(1, 2 * RAMH):
        window = window + padded[:, offset:offset + total_blocks]
    global_block = jnp.arange(total_blocks, dtype=jnp.int32)
    counted = (jnp.minimum(global_block + RAMH, total_blocks) - jnp.maximum(global_block - RAMH, 0)).astype(jnp.float32)
    running = window / (RB * counted)
    normalized = (pieces / (running[:, :, None] + EPS_MEAN)).reshape(STATIONS, SAMPLES).astype(jnp.bfloat16)
    station_hops = normalized.reshape(STATIONS, SAMPLES // HOP, HOP)
    matrix = dft_table()
    smoother = smooth_table()

    def per_block(block_index):
        hops_here = lax.dynamic_slice_in_dim(station_hops, block_index * STN_DEV, STN_DEV, 0)
        group_row = lax.dynamic_slice_in_dim(station_group, block_index * STN_DEV, STN_DEV, 0)
        segments = jnp.concatenate([hops_here[:, :-1], hops_here[:, 1:]], axis=2).reshape(STN_DEV * NSEG, SEGLEN)
        spectra = jnp.dot(segments, matrix, preferred_element_type=jnp.float32)
        whitened = whiten(spectra, smoother)
        member = (group_row[None, :] == jnp.arange(SUB, dtype=jnp.int32)[:, None]).astype(jnp.bfloat16)
        beam_sums = jnp.dot(member, whitened.reshape(STN_DEV, NSEG * 2 * NBIN), preferred_element_type=jnp.float32)
        return beam_sums.astype(jnp.bfloat16).reshape(SUB, NSEG, 2, NBIN)
    beams = lax.map(per_block, jnp.arange(NBLK, dtype=jnp.int32))

    def per_pair(block_index):
        partner_row = partner_blocks[block_index]
        others = beams[jnp.clip(partner_row, 0, NBLK - 1)]
        stacked = cross_terms(beams[block_index], others)
        stacked = jnp.where(partner_row[:, None, None] >= 0, stacked, jnp.float32(0.0))
        return stacked / NSEG
    return lax.map(per_pair, jnp.arange(NBLK, dtype=jnp.int32))
```

```python
import functools
import math

import jax
import jax.numpy as jnp
import numpy as np
from jax import lax
from jax.experimental import pallas as pl
from jax.experimental.pallas import tpu as pltpu
from jax.sharding import PartitionSpec as P

SEGLEN = 4096
HOP = 2048
NBIN = 512
RB = 128
RAMH = 10
SMOOTH = 8
SUB = 16
MAXP = 3
PAD = 16
LANES = 128
CHUNK = 2 * LANES
CHUNKS = 2 * NBIN // CHUNK
VMEM_BYTES = 54000 * 1024

EPS_MEAN = 1e-06
LEVEL = 0.05
MESH = pl.DeviceIdType.MESH


def dft_table():
    sample = np.arange(SEGLEN)
    angles = (sample[:, None] * np.arange(1, NBIN + 1)[None, :] % SEGLEN) * (2.0 * math.pi / SEGLEN)
    taper = (0.5 - 0.5 * np.cos(sample * (2.0 * math.pi / SEGLEN)))[:, None]
    parts = np.stack([taper * np.cos(angles), -taper * np.sin(angles)])
    parts = parts.reshape(2, 2, HOP, CHUNKS, LANES).transpose(1, 3, 2, 0, 4)
    matrix = parts.reshape(2, CHUNKS, HOP, CHUNK)
    return jnp.asarray(matrix.astype(np.float32).astype(jnp.bfloat16))


def whiten(spectra, near):
    starts = range(0, 2 * NBIN, CHUNK)
    real_part = jnp.concatenate([spectra[:, at : at + LANES] for at in starts], axis=1)
    imag_part = jnp.concatenate([spectra[:, at + LANES : at + CHUNK] for at in starts], axis=1)
    powers = real_part * real_part + imag_part * imag_part
    bins = lax.broadcasted_iota(jnp.int32, (1, NBIN), 1)
    count = jnp.minimum(bins + SMOOTH, NBIN - 1) - jnp.maximum(bins - SMOOTH, 0) + 1
    high = powers.astype(jnp.bfloat16)
    rest = (powers - high.astype(jnp.float32)).astype(jnp.bfloat16)
    total = jnp.dot(high, near, preferred_element_type=jnp.float32) + jnp.dot(
        rest, near, preferred_element_type=jnp.float32
    )
    smooth = total * (1.0 / count.astype(jnp.float32))
    floor_level = jnp.sum(powers, axis=1, keepdims=True) * (1.0 / NBIN) + 1e-06
    scale = lax.rsqrt(smooth + LEVEL * floor_level)
    return jnp.concatenate([real_part * scale, imag_part * scale], axis=1).astype(jnp.bfloat16)


def spectra_kernel(
    slabs,
    groups,
    near_rows,
    raw_hbm,
    group_hbm,
    partner_hbm,
    table_hbm,
    out_ref,
    raw_ref,
    group_ref,
    partner_ref,
    table,
    nearby,
    sums,
    halo,
    norm,
    own,
    keep,
    near_out,
    far_out,
    near_in,
    far_in,
    outbox,
    inbox,
    spread_whole,
    spread_split,
    gathered_whole,
    gathered_split,
    mine,
    other,
    raw_sem,
    table_sem,
    argument_sem,
    sum_send,
    sum_recv,
    hop_send,
    hop_recv,
    mix_send,
    mix_recv,
    all_send,
    all_recv,
):
    stations, samples = raw_ref.shape
    blocks = samples // RB
    bins = NBIN // slabs
    t = lax.axis_index("tchunk")
    b = lax.axis_index("stn")
    has_next = t < slabs - 1
    has_prev = t > 0
    nxt = jnp.minimum(t + 1, slabs - 1)
    prv = jnp.maximum(t - 1, 0)

    chunk = samples // 4
    loads = []
    for part in range(4):
        columns = slice(part * chunk, (part + 1) * chunk)
        load = pltpu.make_async_copy(
            raw_hbm.at[:, columns], raw_ref.at[:, columns], raw_sem.at[part]
        )
        load.start()
        loads.append(load)
    fetches = [
        [
            pltpu.make_async_copy(
                table_hbm.at[side, part], table.at[side, part], table_sem.at[side, part]
            )
            for part in range(CHUNKS)
        ]
        for side in range(2)
    ]
    argument_loads = (
        pltpu.make_async_copy(group_hbm, group_ref, argument_sem.at[0]),
        pltpu.make_async_copy(partner_hbm, partner_ref, argument_sem.at[1]),
    )
    for load in argument_loads:
        load.start()
    for part in range(CHUNKS):
        for side in range(2):
            fetches[side][part].start()

    barrier = pltpu.get_barrier_semaphore()
    for step in range(1, slabs):
        pl.semaphore_signal(
            barrier, inc=1, device_id={"tchunk": lax.rem(t + step, slabs)}, device_id_type=MESH
        )
    for step in range(1, groups):
        pl.semaphore_signal(
            barrier, inc=1, device_id={"stn": lax.rem(b + step, groups)}, device_id_type=MESH
        )

    wide = sums.shape[1]
    lane = lax.broadcasted_iota(jnp.int32, (stations, LANES), 1)
    acc = jnp.zeros((stations, LANES), jnp.float32)
    for block in range(blocks):
        if block * RB % chunk == 0:
            loads[block * RB // chunk].wait()
        part = jnp.sum(jnp.abs(raw_ref[:, block * RB : (block + 1) * RB]), axis=1, keepdims=True)
        acc = jnp.where(lane == block, part, acc)
    tall = jnp.concatenate([acc, jnp.zeros((wide - stations, LANES), jnp.float32)], axis=0)
    sums[0:PAD, :] = jnp.zeros((PAD, wide), jnp.float32)
    sums[PAD : PAD + blocks, :] = tall.T[:blocks, :]
    sums[PAD + blocks : 2 * PAD + blocks, :] = jnp.zeros((PAD, wide), jnp.float32)

    pl.semaphore_wait(barrier, slabs - 1 + groups - 1)

    def remote(source, target, sends, recvs, index, place):
        return pltpu.make_async_remote_copy(
            src_ref=source,
            dst_ref=target,
            send_sem=sends.at[index],
            recv_sem=recvs.at[index],
            device_id=place,
            device_id_type=MESH,
        )

    up = {"tchunk": nxt}
    down = {"tchunk": prv}
    sums_up = remote(sums.at[blocks : blocks + PAD, :], halo.at[0], sum_send, sum_recv, 0, up)
    sums_down = remote(sums.at[PAD : 2 * PAD, :], halo.at[1], sum_send, sum_recv, 1, down)

    @pl.when(has_next)
    def _():
        sums_up.start()

    @pl.when(has_prev)
    def _():
        sums_down.start()

    def inverses():
        window = sums[PAD - RAMH : PAD - RAMH + blocks, :]
        for offset in range(1, 2 * RAMH):
            window = window + sums[PAD - RAMH + offset : PAD - RAMH + offset + blocks, :]
        here = t * blocks + lax.broadcasted_iota(jnp.int32, (blocks, wide), 0)
        counted = jnp.minimum(here + RAMH, blocks * slabs) - jnp.maximum(here - RAMH, 0)
        running = window / (RB * counted.astype(jnp.float32))
        inverse = 1.0 / (running + EPS_MEAN)
        return jnp.concatenate(
            [inverse, jnp.zeros((LANES - blocks, wide), jnp.float32)], axis=0
        ).T[:stations, :]

    def normalize(inverse, chosen):
        for block in chosen:
            columns = slice(block * RB, (block + 1) * RB)
            norm[:, columns] = (raw_ref[:, columns] * inverse[:, block : block + 1]).astype(
                jnp.bfloat16
            )

    first, last = RAMH, blocks - RAMH + 1
    normalize(inverses(), range(first, last))

    @pl.when(jnp.logical_not(has_prev))
    def _():
        far_in[...] = jnp.zeros_like(far_in)

    @pl.when(jnp.logical_not(has_next))
    def _():
        near_in[...] = jnp.zeros_like(near_in)

    @pl.when(has_prev)
    def _():
        sums_up.wait_recv()
        sums[0:PAD, :] = halo[0]

    @pl.when(has_next)
    def _():
        sums_down.wait_recv()
        sums[PAD + blocks : 2 * PAD + blocks, :] = halo[1]

    normalize(inverses(), [*range(first), *range(last, blocks)])

    row = lax.broadcasted_iota(jnp.int32, (NBIN, NBIN), 0)
    col = lax.broadcasted_iota(jnp.int32, (NBIN, NBIN), 1)
    nearby[...] = (jnp.abs(row - col) <= SMOOTH).astype(jnp.float32).astype(jnp.bfloat16)
    for load in argument_loads:
        load.wait()
    member = (
        group_ref[...] == lax.broadcasted_iota(jnp.int32, (SUB, stations), 0)
    ).astype(jnp.float32)

    def put_beams(pieces, spectra, members):
        sums_here = jnp.dot(
            members.astype(jnp.bfloat16),
            whiten(spectra, nearby[...]),
            preferred_element_type=jnp.float32,
        ).astype(jnp.bfloat16)
        for index, piece in enumerate(pieces):
            rows = slice(index * SUB, (index + 1) * SUB)
            for part in range(2):
                for slab in range(slabs):
                    begin = part * NBIN + slab * bins
                    outbox[piece, slab, part] = sums_here[rows, begin : begin + bins]
        copies = []
        for step in range(slabs - 1, 0, -1):
            to = lax.rem(t + step, slabs)
            for piece in pieces:
                copy = remote(
                    outbox.at[piece, to],
                    inbox.at[piece, t],
                    mix_send,
                    mix_recv,
                    piece * (slabs - 1) + step - 1,
                    {"tchunk": to},
                )
                copy.start()
                copies.append(copy)
        for piece in pieces:
            inbox[piece, t] = outbox[piece, t]
        return copies

    spreads = (spread_whole, spread_split)
    gathers = (gathered_whole, gathered_split)

    def share(half):
        copies = []
        for step in range(1, groups):
            copy = remote(
                spreads[half],
                gathers[half].at[b],
                all_send,
                all_recv,
                half * (groups - 1) + step - 1,
                {"stn": lax.rem(b + step, groups)},
            )
            copy.start()
            copies.append(copy)
        gathers[half][b] = spreads[half][...]
        return copies

    pairs = SUB * SUB
    pair_row = lax.broadcasted_iota(jnp.int32, (SUB, pairs), 0)
    pair_col = lax.broadcasted_iota(jnp.int32, (SUB, pairs), 1)
    left_hot = (pair_col // SUB == pair_row).astype(jnp.float32).astype(jnp.bfloat16)
    right_hot = (pair_col % SUB == pair_row).astype(jnp.float32).astype(jnp.bfloat16)

    def expand(beams, hot):
        return lax.dot_general(
            beams, hot, (((0,), (0,)), ((), ())), preferred_element_type=jnp.float32
        )

    def expand_mine(half):
        for index in range(spreads[half].shape[0]):
            mine[index] = expand(spreads[half][index], left_hot)

    def stack(half):
        count = spreads[half].shape[0]
        tile = 8
        for slot in range(MAXP):
            partner = partner_ref[0, slot]
            chosen = jnp.maximum(partner, 0)
            weight = jnp.where(partner >= 0, 1.0 / (2 * slabs - 1), 0.0)
            for index in range(count):
                other[slot, index] = expand(gathers[half][chosen, index], right_hot)

            @pl.loop(0, bins // tile)
            def _(step):
                rows = pl.ds(pl.multiple_of(step * tile, tile), tile)
                if half == 0:
                    real_sum = jnp.zeros((tile, pairs), jnp.float32)
                    imag_sum = jnp.zeros((tile, pairs), jnp.float32)
                else:
                    real_sum = out_ref[0, slot, rows, 0:pairs]
                    imag_sum = out_ref[0, slot, rows, pairs : 2 * pairs]
                for segment in range(count // 2):
                    a = mine[2 * segment, rows]
                    c = mine[2 * segment + 1, rows]
                    d = other[slot, 2 * segment, rows]
                    e = other[slot, 2 * segment + 1, rows]
                    real_sum = real_sum + a * d + c * e
                    imag_sum = imag_sum + c * d - a * e
                if half == 1:
                    real_sum = real_sum * weight
                    imag_sum = imag_sum * weight
                out_ref[0, slot, rows, 0:pairs] = real_sum
                out_ref[0, slot, rows, pairs : 2 * pairs] = imag_sum

    def dot(left, right):
        return jnp.dot(left, right, preferred_element_type=jnp.float32)

    near_copies = []
    far_copies = []
    for part in range(CHUNKS):
        columns = slice(part * CHUNK, (part + 1) * CHUNK)
        fetches[0][part].wait()
        opening = dot(norm[:, HOP:], table[0, part])
        far_out[part] = opening[near_rows:].astype(jnp.bfloat16)
        keep[:near_rows, columns] = opening[:near_rows]
        far_copies.append(remote(far_out.at[part], far_in.at[part], hop_send, hop_recv, part, up))
        pl.when(has_next)(far_copies[-1].start)
        fetches[1][part].wait()
        closing = dot(norm[:, :HOP], table[1, part])
        near_out[part] = closing[:near_rows].astype(jnp.bfloat16)
        keep[near_rows:, columns] = closing[near_rows:]
        near_copies.append(
            remote(near_out.at[part], near_in.at[part], hop_send, hop_recv, CHUNKS + part, down)
        )
        pl.when(has_prev)(near_copies[-1].start)

    for part in range(CHUNKS):
        columns = slice(part * CHUNK, (part + 1) * CHUNK)
        own[:, columns] = dot(norm[:, :HOP], table[0, part]) + dot(norm[:, HOP:], table[1, part])
    mixes = put_beams((0,), own[...], member)

    @pl.when(has_next)
    def _():
        for copy in near_copies:
            copy.wait_recv()

    @pl.when(has_prev)
    def _():
        for copy in far_copies:
            copy.wait_recv()

    for part in range(CHUNKS):
        columns = slice(part * CHUNK, (part + 1) * CHUNK)
        own[:near_rows, columns] = keep[:near_rows, columns] + near_in[part].astype(jnp.float32)
        own[near_rows:, columns] = keep[near_rows:, columns] + far_in[part].astype(jnp.float32)
    station = lax.broadcasted_iota(jnp.int32, (SUB, stations), 1)
    split_member = jnp.concatenate(
        [jnp.where(station < near_rows, member, 0.0), jnp.where(station < near_rows, 0.0, member)],
        axis=0,
    )
    split_mixes = put_beams((1, 2), own[...], split_member)

    for copy in mixes:
        copy.wait()
    for slab in range(slabs):
        for part in range(2):
            spread_whole[2 * slab + part] = inbox[0, slab, part]
    whole_shares = share(0)
    expand_mine(0)

    for copy in split_mixes:
        copy.wait()
    for slab in range(slabs - 1):
        for part in range(2):
            both = inbox[1, slab, part].astype(jnp.float32)
            both = both + inbox[2, slab + 1, part].astype(jnp.float32)
            spread_split[2 * slab + part] = both.astype(jnp.bfloat16)
    split_shares = share(1)

    for copy in whole_shares:
        copy.wait()
    stack(0)
    expand_mine(1)

    @pl.when(has_next)
    def _():
        sums_up.wait_send()
        for copy in far_copies:
            copy.wait_send()

    @pl.when(has_prev)
    def _():
        sums_down.wait_send()
        for copy in near_copies:
            copy.wait_send()

    for copy in split_shares:
        copy.wait()
    stack(1)


def body(raw_data, station_group, partner_blocks):
    stations, samples = raw_data.shape
    slabs = lax.axis_size("tchunk")
    groups = lax.axis_size("stn")
    bins = NBIN // slabs
    blocks = samples // RB
    near_rows = -(-stations // 32) * 16
    wide = -(-stations // LANES) * LANES
    vmem = pl.BlockSpec(memory_space=pltpu.VMEM)
    dma = pltpu.SemaphoreType.DMA
    pairs = SUB * SUB
    whole_shape = (2 * slabs, SUB, bins)
    split_shape = (2 * slabs - 2, SUB, bins)
    far = pl.BlockSpec(memory_space=pltpu.HBM)
    return pl.pallas_call(
        functools.partial(spectra_kernel, slabs, groups, near_rows),
        out_shape=jax.ShapeDtypeStruct((1, MAXP, bins, 2 * pairs), jnp.float32),
        in_specs=[far, far, far, far],
        out_specs=vmem,
        scratch_shapes=[
            pltpu.VMEM((stations, samples), jnp.float32),
            pltpu.VMEM((1, stations), jnp.int32),
            pltpu.SMEM((1, MAXP), jnp.int32),
            pltpu.VMEM((2, CHUNKS, HOP, CHUNK), jnp.bfloat16),
            pltpu.VMEM((NBIN, NBIN), jnp.bfloat16),
            pltpu.VMEM((2 * PAD + blocks, wide), jnp.float32),
            pltpu.VMEM((2, PAD, wide), jnp.float32),
            pltpu.VMEM((stations, samples), jnp.bfloat16),
            pltpu.VMEM((stations, 2 * NBIN), jnp.float32),
            pltpu.VMEM((stations, 2 * NBIN), jnp.float32),
            pltpu.VMEM((CHUNKS, near_rows, CHUNK), jnp.bfloat16),
            pltpu.VMEM((CHUNKS, stations - near_rows, CHUNK), jnp.bfloat16),
            pltpu.VMEM((CHUNKS, near_rows, CHUNK), jnp.bfloat16),
            pltpu.VMEM((CHUNKS, stations - near_rows, CHUNK), jnp.bfloat16),
            pltpu.VMEM((3, slabs, 2, SUB, bins), jnp.bfloat16),
            pltpu.VMEM((3, slabs, 2, SUB, bins), jnp.bfloat16),
            pltpu.VMEM(whole_shape, jnp.bfloat16),
            pltpu.VMEM(split_shape, jnp.bfloat16),
            pltpu.VMEM((groups,) + whole_shape, jnp.bfloat16),
            pltpu.VMEM((groups,) + split_shape, jnp.bfloat16),
            pltpu.VMEM((2 * slabs, bins, pairs), jnp.float32),
            pltpu.VMEM((MAXP, 2 * slabs, bins, pairs), jnp.float32),
            dma((4,)),
            dma((2, CHUNKS)),
            dma((2,)),
            dma((2,)),
            dma((2,)),
            dma((2 * CHUNKS,)),
            dma((2 * CHUNKS,)),
            dma((3 * (slabs - 1),)),
            dma((3 * (slabs - 1),)),
            dma((2 * (groups - 1),)),
            dma((2 * (groups - 1),)),
        ],
        compiler_params=pltpu.CompilerParams(
            collective_id=0, has_side_effects=True, vmem_limit_bytes=VMEM_BYTES
        ),
    )(raw_data, station_group[None, :], partner_blocks, dft_table())


def solution(mesh):
    placed = (P("stn", ("hour", "tchunk")), P("stn"), P("stn", None))
    return jax.shard_map(
        body,
        mesh=mesh,
        in_specs=placed,
        out_specs=P(("hour", "stn"), None, "tchunk", None),
        check_vma=False,
    )
```

```python
import functools
import math

import jax
import jax.numpy as jnp
import numpy as np
from jax import lax
from jax.experimental import pallas as pl
from jax.experimental.pallas import tpu as pltpu
from jax.sharding import PartitionSpec as P

SEGLEN = 4096
HOP = 2048
NBIN = 512
RB = 128
RAMH = 10
SMOOTH = 8
SUB = 16
MAXP = 3
PAD = 16
LANES = 128
CHUNK = 2 * LANES
CHUNKS = 2 * NBIN // CHUNK
VMEM_BYTES = 54000 * 1024

EPS_MEAN = 1e-06
LEVEL = 0.05
MESH = pl.DeviceIdType.MESH


def dft_table():
    sample = np.arange(SEGLEN)
    angles = (sample[:, None] * np.arange(1, NBIN + 1)[None, :] % SEGLEN) * (2.0 * math.pi / SEGLEN)
    taper = (0.5 - 0.5 * np.cos(sample * (2.0 * math.pi / SEGLEN)))[:, None]
    parts = np.stack([taper * np.cos(angles), -taper * np.sin(angles)])
    parts = parts.reshape(2, 2, HOP, CHUNKS, LANES).transpose(1, 3, 2, 0, 4)
    matrix = parts.reshape(2, CHUNKS, HOP, CHUNK)
    return jnp.asarray(matrix.astype(np.float32).astype(jnp.bfloat16))


def whiten(spectra, near):
    starts = range(0, 2 * NBIN, CHUNK)
    real_part = jnp.concatenate([spectra[:, at : at + LANES] for at in starts], axis=1)
    imag_part = jnp.concatenate([spectra[:, at + LANES : at + CHUNK] for at in starts], axis=1)
    powers = real_part * real_part + imag_part * imag_part
    bins = lax.broadcasted_iota(jnp.int32, (1, NBIN), 1)
    count = jnp.minimum(bins + SMOOTH, NBIN - 1) - jnp.maximum(bins - SMOOTH, 0) + 1
    high = powers.astype(jnp.bfloat16)
    rest = (powers - high.astype(jnp.float32)).astype(jnp.bfloat16)
    total = jnp.dot(high, near, preferred_element_type=jnp.float32) + jnp.dot(
        rest, near, preferred_element_type=jnp.float32
    )
    smooth = total * (1.0 / count.astype(jnp.float32))
    floor_level = jnp.sum(powers, axis=1, keepdims=True) * (1.0 / NBIN) + 1e-06
    scale = lax.rsqrt(smooth + LEVEL * floor_level)
    return jnp.concatenate([real_part * scale, imag_part * scale], axis=1).astype(jnp.bfloat16)


def spectra_kernel(
    slabs,
    groups,
    near_rows,
    raw_hbm,
    group_hbm,
    partner_hbm,
    table_hbm,
    out_ref,
    raw_ref,
    group_ref,
    partner_ref,
    table,
    nearby,
    sums,
    halo,
    norm,
    own,
    keep,
    near_out,
    far_out,
    near_in,
    far_in,
    outbox,
    inbox,
    spread_whole,
    spread_split,
    gathered_whole,
    gathered_split,
    mine,
    other,
    raw_sem,
    table_sem,
    argument_sem,
    sum_send,
    sum_recv,
    hop_send,
    hop_recv,
    mix_send,
    mix_recv,
    all_send,
    all_recv,
):
    stations, samples = raw_ref.shape
    blocks = samples // RB
    bins = NBIN // slabs
    t = lax.axis_index("tchunk")
    b = lax.axis_index("stn")
    has_next = t < slabs - 1
    has_prev = t > 0
    nxt = jnp.minimum(t + 1, slabs - 1)
    prv = jnp.maximum(t - 1, 0)

    chunk = samples // 4
    loads = []
    for part in range(4):
        columns = slice(part * chunk, (part + 1) * chunk)
        load = pltpu.make_async_copy(
            raw_hbm.at[:, columns], raw_ref.at[:, columns], raw_sem.at[part]
        )
        load.start()
        loads.append(load)
    fetches = [
        [
            pltpu.make_async_copy(
                table_hbm.at[side, part], table.at[side, part], table_sem.at[side, part]
            )
            for part in range(CHUNKS)
        ]
        for side in range(2)
    ]
    argument_loads = (
        pltpu.make_async_copy(group_hbm, group_ref, argument_sem.at[0]),
        pltpu.make_async_copy(partner_hbm, partner_ref, argument_sem.at[1]),
    )
    for load in argument_loads:
        load.start()
    for part in range(CHUNKS):
        for side in range(2):
            fetches[side][part].start()

    barrier = pltpu.get_barrier_semaphore()
    for step in range(1, slabs):
        pl.semaphore_signal(
            barrier, inc=1, device_id={"tchunk": lax.rem(t + step, slabs)}, device_id_type=MESH
        )
    for step in range(1, groups):
        pl.semaphore_signal(
            barrier, inc=1, device_id={"stn": lax.rem(b + step, groups)}, device_id_type=MESH
        )

    wide = sums.shape[1]
    lane = lax.broadcasted_iota(jnp.int32, (stations, LANES), 1)
    acc = jnp.zeros((stations, LANES), jnp.float32)
    for block in range(blocks):
        if block * RB % chunk == 0:
            loads[block * RB // chunk].wait()
        part = jnp.sum(jnp.abs(raw_ref[:, block * RB : (block + 1) * RB]), axis=1, keepdims=True)
        acc = jnp.where(lane == block, part, acc)
    tall = jnp.concatenate([acc, jnp.zeros((wide - stations, LANES), jnp.float32)], axis=0)
    sums[0:PAD, :] = jnp.zeros((PAD, wide), jnp.float32)
    sums[PAD : PAD + blocks, :] = tall.T[:blocks, :]
    sums[PAD + blocks : 2 * PAD + blocks, :] = jnp.zeros((PAD, wide), jnp.float32)

    pl.semaphore_wait(barrier, slabs - 1 + groups - 1)

    def remote(source, target, sends, recvs, index, place):
        return pltpu.make_async_remote_copy(
            src_ref=source,
            dst_ref=target,
            send_sem=sends.at[index],
            recv_sem=recvs.at[index],
            device_id=place,
            device_id_type=MESH,
        )

    up = {"tchunk": nxt}
    down = {"tchunk": prv}
    sums_up = remote(sums.at[blocks : blocks + PAD, :], halo.at[0], sum_send, sum_recv, 0, up)
    sums_down = remote(sums.at[PAD : 2 * PAD, :], halo.at[1], sum_send, sum_recv, 1, down)

    @pl.when(has_next)
    def _():
        sums_up.start()

    @pl.when(has_prev)
    def _():
        sums_down.start()

    def inverses():
        window = sums[PAD - RAMH : PAD - RAMH + blocks, :]
        for offset in range(1, 2 * RAMH):
            window = window + sums[PAD - RAMH + offset : PAD - RAMH + offset + blocks, :]
        here = t * blocks + lax.broadcasted_iota(jnp.int32, (blocks, wide), 0)
        counted = jnp.minimum(here + RAMH, blocks * slabs) - jnp.maximum(here - RAMH, 0)
        running = window / (RB * counted.astype(jnp.float32))
        inverse = 1.0 / (running + EPS_MEAN)
        return jnp.concatenate(
            [inverse, jnp.zeros((LANES - blocks, wide), jnp.float32)], axis=0
        ).T[:stations, :]

    def normalize(inverse, chosen):
        for block in chosen:
            columns = slice(block * RB, (block + 1) * RB)
            rows = slice(block * RB // HOP * stations, (block * RB // HOP + 1) * stations)
            place = slice(block * RB % HOP, block * RB % HOP + RB)
            norm[rows, place] = (raw_ref[:, columns] * inverse[:, block : block + 1]).astype(
                jnp.bfloat16
            )

    first, last = RAMH, blocks - RAMH + 1
    normalize(inverses(), range(first, last))

    @pl.when(jnp.logical_not(has_prev))
    def _():
        far_in[...] = jnp.zeros_like(far_in)

    @pl.when(jnp.logical_not(has_next))
    def _():
        near_in[...] = jnp.zeros_like(near_in)

    @pl.when(has_prev)
    def _():
        sums_up.wait_recv()
        sums[0:PAD, :] = halo[0]

    @pl.when(has_next)
    def _():
        sums_down.wait_recv()
        sums[PAD + blocks : 2 * PAD + blocks, :] = halo[1]

    normalize(inverses(), [*range(first), *range(last, blocks)])

    row = lax.broadcasted_iota(jnp.int32, (NBIN, NBIN), 0)
    col = lax.broadcasted_iota(jnp.int32, (NBIN, NBIN), 1)
    nearby[...] = (jnp.abs(row - col) <= SMOOTH).astype(jnp.float32).astype(jnp.bfloat16)
    for load in argument_loads:
        load.wait()
    member = (
        group_ref[...] == lax.broadcasted_iota(jnp.int32, (SUB, stations), 0)
    ).astype(jnp.float32)

    def put_beams(pieces, spectra, members):
        sums_here = jnp.dot(
            members.astype(jnp.bfloat16),
            whiten(spectra, nearby[...]),
            preferred_element_type=jnp.float32,
        ).astype(jnp.bfloat16)
        for index, piece in enumerate(pieces):
            rows = slice(index * SUB, (index + 1) * SUB)
            for part in range(2):
                for slab in range(slabs):
                    begin = part * NBIN + slab * bins
                    outbox[piece, slab, part] = sums_here[rows, begin : begin + bins]
        copies = []
        for step in range(slabs - 1, 0, -1):
            to = lax.rem(t + step, slabs)
            for piece in pieces:
                copy = remote(
                    outbox.at[piece, to],
                    inbox.at[piece, t],
                    mix_send,
                    mix_recv,
                    piece * (slabs - 1) + step - 1,
                    {"tchunk": to},
                )
                copy.start()
                copies.append(copy)
        for piece in pieces:
            inbox[piece, t] = outbox[piece, t]
        return copies

    spreads = (spread_whole, spread_split)
    gathers = (gathered_whole, gathered_split)

    def share(half):
        copies = []
        for step in range(1, groups):
            copy = remote(
                spreads[half],
                gathers[half].at[b],
                all_send,
                all_recv,
                half * (groups - 1) + step - 1,
                {"stn": lax.rem(b + step, groups)},
            )
            copy.start()
            copies.append(copy)
        gathers[half][b] = spreads[half][...]
        return copies

    pairs = SUB * SUB
    pair_row = lax.broadcasted_iota(jnp.int32, (SUB, pairs), 0)
    pair_col = lax.broadcasted_iota(jnp.int32, (SUB, pairs), 1)
    left_hot = (pair_col // SUB == pair_row).astype(jnp.float32).astype(jnp.bfloat16)
    right_hot = (pair_col % SUB == pair_row).astype(jnp.float32).astype(jnp.bfloat16)

    def expand(beams, hot):
        return lax.dot_general(
            beams, hot, (((0,), (0,)), ((), ())), preferred_element_type=jnp.float32
        )

    def expand_mine(half):
        for index in range(spreads[half].shape[0]):
            mine[index] = expand(spreads[half][index], left_hot)

    def stack(half):
        count = spreads[half].shape[0]
        tile = 8
        for slot in range(MAXP):
            partner = partner_ref[0, slot]
            chosen = jnp.maximum(partner, 0)
            weight = jnp.where(partner >= 0, 1.0 / (2 * slabs - 1), 0.0)
            for index in range(count):
                other[slot, index] = expand(gathers[half][chosen, index], right_hot)

            for step in range(bins // tile):
                rows = slice(step * tile, (step + 1) * tile)
                if half == 0:
                    real_sum = jnp.zeros((tile, pairs), jnp.float32)
                    imag_sum = jnp.zeros((tile, pairs), jnp.float32)
                else:
                    real_sum = out_ref[0, slot, rows, 0:pairs]
                    imag_sum = out_ref[0, slot, rows, pairs : 2 * pairs]
                for segment in range(count // 2):
                    a = mine[2 * segment, rows]
                    c = mine[2 * segment + 1, rows]
                    d = other[slot, 2 * segment, rows]
                    e = other[slot, 2 * segment + 1, rows]
                    real_sum = real_sum + a * d + c * e
                    imag_sum = imag_sum + c * d - a * e
                if half == 1:
                    real_sum = real_sum * weight
                    imag_sum = imag_sum * weight
                out_ref[0, slot, rows, 0:pairs] = real_sum
                out_ref[0, slot, rows, pairs : 2 * pairs] = imag_sum

    def dot(left, right):
        return jnp.dot(left, right, preferred_element_type=jnp.float32)

    near_copies = []
    far_copies = []
    for part in range(CHUNKS):
        columns = slice(part * CHUNK, (part + 1) * CHUNK)
        fetches[0][part].wait()
        fetches[1][part].wait()
        opening = dot(norm[stations:], table[0, part])
        closing = dot(norm[:stations], table[1, part])
        far_out[part] = opening[near_rows:].astype(jnp.bfloat16)
        near_out[part] = closing[:near_rows].astype(jnp.bfloat16)
        keep[:near_rows, columns] = opening[:near_rows]
        keep[near_rows:, columns] = closing[near_rows:]
        far_copies.append(remote(far_out.at[part], far_in.at[part], hop_send, hop_recv, part, up))
        near_copies.append(
            remote(near_out.at[part], near_in.at[part], hop_send, hop_recv, CHUNKS + part, down)
        )
        pl.when(has_next)(far_copies[-1].start)
        pl.when(has_prev)(near_copies[-1].start)

    for part in range(CHUNKS):
        columns = slice(part * CHUNK, (part + 1) * CHUNK)
        own[:, columns] = dot(norm[:stations], table[0, part]) + dot(norm[stations:], table[1, part])
    mixes = put_beams((0,), own[...], member)

    @pl.when(has_next)
    def _():
        for copy in near_copies:
            copy.wait_recv()

    @pl.when(has_prev)
    def _():
        for copy in far_copies:
            copy.wait_recv()

    for part in range(CHUNKS):
        columns = slice(part * CHUNK, (part + 1) * CHUNK)
        own[:near_rows, columns] = keep[:near_rows, columns] + near_in[part].astype(jnp.float32)
        own[near_rows:, columns] = keep[near_rows:, columns] + far_in[part].astype(jnp.float32)
    station = lax.broadcasted_iota(jnp.int32, (SUB, stations), 1)
    split_member = jnp.concatenate(
        [jnp.where(station < near_rows, member, 0.0), jnp.where(station < near_rows, 0.0, member)],
        axis=0,
    )
    split_mixes = put_beams((1, 2), own[...], split_member)

    for copy in mixes:
        copy.wait()
    for slab in range(slabs):
        for part in range(2):
            spread_whole[2 * slab + part] = inbox[0, slab, part]
    whole_shares = share(0)
    expand_mine(0)

    for copy in split_mixes:
        copy.wait()
    for slab in range(slabs - 1):
        for part in range(2):
            both = inbox[1, slab, part].astype(jnp.float32)
            both = both + inbox[2, slab + 1, part].astype(jnp.float32)
            spread_split[2 * slab + part] = both.astype(jnp.bfloat16)
    split_shares = share(1)

    for copy in whole_shares:
        copy.wait()
    stack(0)
    expand_mine(1)

    @pl.when(has_next)
    def _():
        sums_up.wait_send()
        for copy in far_copies:
            copy.wait_send()

    @pl.when(has_prev)
    def _():
        sums_down.wait_send()
        for copy in near_copies:
            copy.wait_send()

    for copy in split_shares:
        copy.wait()
    stack(1)


def body(raw_data, station_group, partner_blocks):
    stations, samples = raw_data.shape
    slabs = lax.axis_size("tchunk")
    groups = lax.axis_size("stn")
    bins = NBIN // slabs
    blocks = samples // RB
    near_rows = -(-stations // 32) * 16
    wide = -(-stations // LANES) * LANES
    vmem = pl.BlockSpec(memory_space=pltpu.VMEM)
    dma = pltpu.SemaphoreType.DMA
    pairs = SUB * SUB
    whole_shape = (2 * slabs, SUB, bins)
    split_shape = (2 * slabs - 2, SUB, bins)
    far = pl.BlockSpec(memory_space=pltpu.HBM)
    return pl.pallas_call(
        functools.partial(spectra_kernel, slabs, groups, near_rows),
        out_shape=jax.ShapeDtypeStruct((1, MAXP, bins, 2 * pairs), jnp.float32),
        in_specs=[far, far, far, far],
        out_specs=vmem,
        scratch_shapes=[
            pltpu.VMEM((stations, samples), jnp.float32),
            pltpu.VMEM((1, stations), jnp.int32),
            pltpu.SMEM((1, MAXP), jnp.int32),
            pltpu.VMEM((2, CHUNKS, HOP, CHUNK), jnp.bfloat16),
            pltpu.VMEM((NBIN, NBIN), jnp.bfloat16),
            pltpu.VMEM((2 * PAD + blocks, wide), jnp.float32),
            pltpu.VMEM((2, PAD, wide), jnp.float32),
            pltpu.VMEM((2 * stations, HOP), jnp.bfloat16),
            pltpu.VMEM((stations, 2 * NBIN), jnp.float32),
            pltpu.VMEM((stations, 2 * NBIN), jnp.float32),
            pltpu.VMEM((CHUNKS, near_rows, CHUNK), jnp.bfloat16),
            pltpu.VMEM((CHUNKS, stations - near_rows, CHUNK), jnp.bfloat16),
            pltpu.VMEM((CHUNKS, near_rows, CHUNK), jnp.bfloat16),
            pltpu.VMEM((CHUNKS, stations - near_rows, CHUNK), jnp.bfloat16),
            pltpu.VMEM((3, slabs, 2, SUB, bins), jnp.bfloat16),
            pltpu.VMEM((3, slabs, 2, SUB, bins), jnp.bfloat16),
            pltpu.VMEM(whole_shape, jnp.bfloat16),
            pltpu.VMEM(split_shape, jnp.bfloat16),
            pltpu.VMEM((groups,) + whole_shape, jnp.bfloat16),
            pltpu.VMEM((groups,) + split_shape, jnp.bfloat16),
            pltpu.VMEM((2 * slabs, bins, pairs), jnp.float32),
            pltpu.VMEM((MAXP, 2 * slabs, bins, pairs), jnp.float32),
            dma((4,)),
            dma((2, CHUNKS)),
            dma((2,)),
            dma((2,)),
            dma((2,)),
            dma((2 * CHUNKS,)),
            dma((2 * CHUNKS,)),
            dma((3 * (slabs - 1),)),
            dma((3 * (slabs - 1),)),
            dma((2 * (groups - 1),)),
            dma((2 * (groups - 1),)),
        ],
        compiler_params=pltpu.CompilerParams(
            collective_id=0, has_side_effects=True, vmem_limit_bytes=VMEM_BYTES
        ),
    )(raw_data, pltpu.with_memory_space_constraint(station_group[None, :], pltpu.HBM), pltpu.with_memory_space_constraint(partner_blocks, pltpu.HBM), dft_table())


def solution(mesh):
    placed = (P("stn", ("hour", "tchunk")), P("stn"), P("stn", None))
    return jax.shard_map(
        body,
        mesh=mesh,
        in_specs=placed,
        out_specs=P(("hour", "stn"), None, "tchunk", None),
        check_vma=False,
    )
```

```python
import functools
import math

import jax
import jax.numpy as jnp
import numpy as np
from jax import lax
from jax.experimental import pallas as pl
from jax.experimental.pallas import tpu as pltpu
from jax.sharding import PartitionSpec as P

SEGLEN = 4096
HOP = 2048
NBIN = 512
RB = 128
RAMH = 10
SMOOTH = 8
SUB = 16
MAXP = 3
PAD = 16
LANES = 128
CHUNK = 2 * LANES
CHUNKS = 2 * NBIN // CHUNK
VMEM_BYTES = 54000 * 1024

EPS_MEAN = 1e-06
LEVEL = 0.05
MESH = pl.DeviceIdType.MESH


def dft_table():
    sample = np.arange(SEGLEN)
    angles = (sample[:, None] * np.arange(1, NBIN + 1)[None, :] % SEGLEN) * (2.0 * math.pi / SEGLEN)
    taper = (0.5 - 0.5 * np.cos(sample * (2.0 * math.pi / SEGLEN)))[:, None]
    parts = np.stack([taper * np.cos(angles), -taper * np.sin(angles)])
    parts = parts.reshape(2, 2, HOP, CHUNKS, LANES).transpose(1, 3, 2, 0, 4)
    matrix = parts.reshape(2, CHUNKS, HOP, CHUNK)
    return jnp.asarray(matrix.astype(np.float32).astype(jnp.bfloat16))


def whiten(spectra, near):
    starts = range(0, 2 * NBIN, CHUNK)
    real_part = jnp.concatenate([spectra[:, at : at + LANES] for at in starts], axis=1)
    imag_part = jnp.concatenate([spectra[:, at + LANES : at + CHUNK] for at in starts], axis=1)
    powers = real_part * real_part + imag_part * imag_part
    bins = lax.broadcasted_iota(jnp.int32, (1, NBIN), 1)
    count = jnp.minimum(bins + SMOOTH, NBIN - 1) - jnp.maximum(bins - SMOOTH, 0) + 1
    high = powers.astype(jnp.bfloat16)
    rest = (powers - high.astype(jnp.float32)).astype(jnp.bfloat16)
    total = jnp.dot(high, near, preferred_element_type=jnp.float32) + jnp.dot(
        rest, near, preferred_element_type=jnp.float32
    )
    smooth = total * (1.0 / count.astype(jnp.float32))
    floor_level = jnp.sum(powers, axis=1, keepdims=True) * (1.0 / NBIN) + 1e-06
    scale = lax.rsqrt(smooth + LEVEL * floor_level)
    return jnp.concatenate([real_part * scale, imag_part * scale], axis=1).astype(jnp.bfloat16)


def spectra_kernel(
    slabs,
    groups,
    near_rows,
    raw_hbm,
    group_hbm,
    partner_hbm,
    table_hbm,
    out_ref,
    raw_ref,
    group_ref,
    partner_ref,
    table,
    nearby,
    sums,
    halo,
    norm,
    own,
    keep,
    near_out,
    far_out,
    near_in,
    far_in,
    outbox,
    inbox,
    spread_whole,
    spread_split,
    gathered_whole,
    gathered_split,
    mine,
    other,
    raw_sem,
    table_sem,
    argument_sem,
    sum_send,
    sum_recv,
    hop_send,
    hop_recv,
    mix_send,
    mix_recv,
    all_send,
    all_recv,
):
    stations, samples = raw_ref.shape
    blocks = samples // RB
    bins = NBIN // slabs
    t = lax.axis_index("tchunk")
    b = lax.axis_index("stn")
    has_next = t < slabs - 1
    has_prev = t > 0
    nxt = jnp.minimum(t + 1, slabs - 1)
    prv = jnp.maximum(t - 1, 0)

    chunk = samples // 4
    loads = []
    for part in range(4):
        columns = slice(part * chunk, (part + 1) * chunk)
        load = pltpu.make_async_copy(
            raw_hbm.at[:, columns], raw_ref.at[:, columns], raw_sem.at[part]
        )
        load.start()
        loads.append(load)
    fetches = [
        [
            pltpu.make_async_copy(
                table_hbm.at[side, part], table.at[side, part], table_sem.at[side, part]
            )
            for part in range(CHUNKS)
        ]
        for side in range(2)
    ]
    argument_loads = (
        pltpu.make_async_copy(group_hbm, group_ref, argument_sem.at[0]),
        pltpu.make_async_copy(partner_hbm, partner_ref, argument_sem.at[1]),
    )

    barrier = pltpu.get_barrier_semaphore()
    for step in range(1, slabs):
        pl.semaphore_signal(
            barrier, inc=1, device_id={"tchunk": lax.rem(t + step, slabs)}, device_id_type=MESH
        )
    for step in range(1, groups):
        pl.semaphore_signal(
            barrier, inc=1, device_id={"stn": lax.rem(b + step, groups)}, device_id_type=MESH
        )

    wide = sums.shape[1]
    lane = lax.broadcasted_iota(jnp.int32, (stations, LANES), 1)
    acc = jnp.zeros((stations, LANES), jnp.float32)
    for block in range(blocks):
        if block * RB % chunk == 0:
            loads[block * RB // chunk].wait()
            if block * RB // chunk == len(loads) - 1:
                for copy in [*(fetches[at % 2][at // 2] for at in range(2 * CHUNKS)), *argument_loads]:
                    copy.start()
        part = jnp.sum(jnp.abs(raw_ref[:, block * RB : (block + 1) * RB]), axis=1, keepdims=True)
        acc = jnp.where(lane == block, part, acc)
    tall = jnp.concatenate([acc, jnp.zeros((wide - stations, LANES), jnp.float32)], axis=0)
    sums[0:PAD, :] = jnp.zeros((PAD, wide), jnp.float32)
    sums[PAD : PAD + blocks, :] = tall.T[:blocks, :]
    sums[PAD + blocks : 2 * PAD + blocks, :] = jnp.zeros((PAD, wide), jnp.float32)

    pl.semaphore_wait(barrier, slabs - 1 + groups - 1)

    def remote(source, target, sends, recvs, index, place):
        return pltpu.make_async_remote_copy(
            src_ref=source,
            dst_ref=target,
            send_sem=sends.at[index],
            recv_sem=recvs.at[index],
            device_id=place,
            device_id_type=MESH,
        )

    up = {"tchunk": nxt}
    down = {"tchunk": prv}
    sums_up = remote(sums.at[blocks : blocks + PAD, :], halo.at[0], sum_send, sum_recv, 0, up)
    sums_down = remote(sums.at[PAD : 2 * PAD, :], halo.at[1], sum_send, sum_recv, 1, down)

    @pl.when(has_next)
    def _():
        sums_up.start()

    @pl.when(has_prev)
    def _():
        sums_down.start()

    def inverses():
        window = sums[PAD - RAMH : PAD - RAMH + blocks, :]
        for offset in range(1, 2 * RAMH):
            window = window + sums[PAD - RAMH + offset : PAD - RAMH + offset + blocks, :]
        here = t * blocks + lax.broadcasted_iota(jnp.int32, (blocks, wide), 0)
        counted = jnp.minimum(here + RAMH, blocks * slabs) - jnp.maximum(here - RAMH, 0)
        running = window / (RB * counted.astype(jnp.float32))
        inverse = 1.0 / (running + EPS_MEAN)
        return jnp.concatenate(
            [inverse, jnp.zeros((LANES - blocks, wide), jnp.float32)], axis=0
        ).T[:stations, :]

    def normalize(inverse, chosen):
        for block in chosen:
            columns = slice(block * RB, (block + 1) * RB)
            rows = slice(block * RB // HOP * stations, (block * RB // HOP + 1) * stations)
            place = slice(block * RB % HOP, block * RB % HOP + RB)
            norm[rows, place] = (raw_ref[:, columns] * inverse[:, block : block + 1]).astype(
                jnp.bfloat16
            )

    first, last = RAMH, blocks - RAMH + 1
    normalize(inverses(), range(first, last))

    @pl.when(jnp.logical_not(has_prev))
    def _():
        far_in[...] = jnp.zeros_like(far_in)

    @pl.when(jnp.logical_not(has_next))
    def _():
        near_in[...] = jnp.zeros_like(near_in)

    @pl.when(has_prev)
    def _():
        sums_up.wait_recv()
        sums[0:PAD, :] = halo[0]

    @pl.when(has_next)
    def _():
        sums_down.wait_recv()
        sums[PAD + blocks : 2 * PAD + blocks, :] = halo[1]

    normalize(inverses(), [*range(first), *range(last, blocks)])

    row = lax.broadcasted_iota(jnp.int32, (NBIN, NBIN), 0)
    col = lax.broadcasted_iota(jnp.int32, (NBIN, NBIN), 1)
    nearby[...] = (jnp.abs(row - col) <= SMOOTH).astype(jnp.float32).astype(jnp.bfloat16)
    for load in argument_loads:
        load.wait()
    member = (
        group_ref[...] == lax.broadcasted_iota(jnp.int32, (SUB, stations), 0)
    ).astype(jnp.float32)

    def put_beams(pieces, spectra, members):
        sums_here = jnp.dot(
            members.astype(jnp.bfloat16),
            whiten(spectra, nearby[...]),
            preferred_element_type=jnp.float32,
        ).astype(jnp.bfloat16)
        for index, piece in enumerate(pieces):
            rows = slice(index * SUB, (index + 1) * SUB)
            for part in range(2):
                for slab in range(slabs):
                    begin = part * NBIN + slab * bins
                    outbox[piece, slab, part] = sums_here[rows, begin : begin + bins]
        copies = []
        for step in range(slabs - 1, 0, -1):
            to = lax.rem(t + step, slabs)
            for piece in pieces:
                copy = remote(
                    outbox.at[piece, to],
                    inbox.at[piece, t],
                    mix_send,
                    mix_recv,
                    piece * (slabs - 1) + step - 1,
                    {"tchunk": to},
                )
                copy.start()
                copies.append(copy)
        for piece in pieces:
            inbox[piece, t] = outbox[piece, t]
        return copies

    spreads = (spread_whole, spread_split)
    gathers = (gathered_whole, gathered_split)

    def share(half):
        copies = []
        for step in range(1, groups):
            copy = remote(
                spreads[half],
                gathers[half].at[b],
                all_send,
                all_recv,
                half * (groups - 1) + step - 1,
                {"stn": lax.rem(b + step, groups)},
            )
            copy.start()
            copies.append(copy)
        gathers[half][b] = spreads[half][...]
        return copies

    pairs = SUB * SUB
    pair_row = lax.broadcasted_iota(jnp.int32, (SUB, pairs), 0)
    pair_col = lax.broadcasted_iota(jnp.int32, (SUB, pairs), 1)
    left_hot = (pair_col // SUB == pair_row).astype(jnp.float32).astype(jnp.bfloat16)
    right_hot = (pair_col % SUB == pair_row).astype(jnp.float32).astype(jnp.bfloat16)

    def expand(beams, hot):
        return lax.dot_general(
            beams, hot, (((0,), (0,)), ((), ())), preferred_element_type=jnp.float32
        )

    def expand_mine(half):
        for index in range(spreads[half].shape[0]):
            mine[index] = expand(spreads[half][index], left_hot)

    def stack(half):
        count = spreads[half].shape[0]
        tile = 8
        for slot in range(MAXP):
            partner = partner_ref[0, slot]
            chosen = jnp.maximum(partner, 0)
            weight = jnp.where(partner >= 0, 1.0 / (2 * slabs - 1), 0.0)
            for index in range(count):
                other[slot, index] = expand(gathers[half][chosen, index], right_hot)

            for step in range(bins // tile):
                rows = slice(step * tile, (step + 1) * tile)
                if half == 0:
                    real_sum = jnp.zeros((tile, pairs), jnp.float32)
                    imag_sum = jnp.zeros((tile, pairs), jnp.float32)
                else:
                    real_sum = out_ref[0, slot, rows, 0:pairs]
                    imag_sum = out_ref[0, slot, rows, pairs : 2 * pairs]
                for segment in range(count // 2):
                    a = mine[2 * segment, rows]
                    c = mine[2 * segment + 1, rows]
                    d = other[slot, 2 * segment, rows]
                    e = other[slot, 2 * segment + 1, rows]
                    real_sum = real_sum + a * d + c * e
                    imag_sum = imag_sum + c * d - a * e
                if half == 1:
                    real_sum = real_sum * weight
                    imag_sum = imag_sum * weight
                out_ref[0, slot, rows, 0:pairs] = real_sum
                out_ref[0, slot, rows, pairs : 2 * pairs] = imag_sum

    def dot(left, right):
        return jnp.dot(left, right, preferred_element_type=jnp.float32)

    near_copies = []
    far_copies = []
    for part in range(CHUNKS):
        columns = slice(part * CHUNK, (part + 1) * CHUNK)
        fetches[0][part].wait()
        fetches[1][part].wait()
        opening = dot(norm[stations:], table[0, part])
        closing = dot(norm[:stations], table[1, part])
        far_out[part] = opening[near_rows:].astype(jnp.bfloat16)
        near_out[part] = closing[:near_rows].astype(jnp.bfloat16)
        keep[:near_rows, columns] = opening[:near_rows]
        keep[near_rows:, columns] = closing[near_rows:]
        far_copies.append(remote(far_out.at[part], far_in.at[part], hop_send, hop_recv, part, up))
        near_copies.append(
            remote(near_out.at[part], near_in.at[part], hop_send, hop_recv, CHUNKS + part, down)
        )
        pl.when(has_next)(far_copies[-1].start)
        pl.when(has_prev)(near_copies[-1].start)

    for part in range(CHUNKS):
        columns = slice(part * CHUNK, (part + 1) * CHUNK)
        own[:, columns] = dot(norm[:stations], table[0, part]) + dot(norm[stations:], table[1, part])
    mixes = put_beams((0,), own[...], member)

    @pl.when(has_next)
    def _():
        for copy in near_copies:
            copy.wait_recv()

    @pl.when(has_prev)
    def _():
        for copy in far_copies:
            copy.wait_recv()

    for part in range(CHUNKS):
        columns = slice(part * CHUNK, (part + 1) * CHUNK)
        own[:near_rows, columns] = keep[:near_rows, columns] + near_in[part].astype(jnp.float32)
        own[near_rows:, columns] = keep[near_rows:, columns] + far_in[part].astype(jnp.float32)
    station = lax.broadcasted_iota(jnp.int32, (SUB, stations), 1)
    split_member = jnp.concatenate(
        [jnp.where(station < near_rows, member, 0.0), jnp.where(station < near_rows, 0.0, member)],
        axis=0,
    )
    split_mixes = put_beams((1, 2), own[...], split_member)

    for copy in mixes:
        copy.wait()
    for slab in range(slabs):
        for part in range(2):
            spread_whole[2 * slab + part] = inbox[0, slab, part]
    whole_shares = share(0)
    expand_mine(0)

    for copy in split_mixes:
        copy.wait()
    for slab in range(slabs - 1):
        for part in range(2):
            both = inbox[1, slab, part].astype(jnp.float32)
            both = both + inbox[2, slab + 1, part].astype(jnp.float32)
            spread_split[2 * slab + part] = both.astype(jnp.bfloat16)
    split_shares = share(1)

    for copy in whole_shares:
        copy.wait()
    stack(0)
    expand_mine(1)

    @pl.when(has_next)
    def _():
        sums_up.wait_send()
        for copy in far_copies:
            copy.wait_send()

    @pl.when(has_prev)
    def _():
        sums_down.wait_send()
        for copy in near_copies:
            copy.wait_send()

    for copy in split_shares:
        copy.wait()
    stack(1)


def body(raw_data, station_group, partner_blocks):
    stations, samples = raw_data.shape
    slabs = lax.axis_size("tchunk")
    groups = lax.axis_size("stn")
    bins = NBIN // slabs
    blocks = samples // RB
    near_rows = -(-stations // 32) * 16
    wide = -(-stations // LANES) * LANES
    vmem = pl.BlockSpec(memory_space=pltpu.VMEM)
    dma = pltpu.SemaphoreType.DMA
    pairs = SUB * SUB
    whole_shape = (2 * slabs, SUB, bins)
    split_shape = (2 * slabs - 2, SUB, bins)
    far = pl.BlockSpec(memory_space=pltpu.HBM)
    return pl.pallas_call(
        functools.partial(spectra_kernel, slabs, groups, near_rows),
        out_shape=jax.ShapeDtypeStruct((1, MAXP, bins, 2 * pairs), jnp.float32),
        in_specs=[far, far, far, far],
        out_specs=vmem,
        scratch_shapes=[
            pltpu.VMEM((stations, samples), jnp.float32),
            pltpu.VMEM((1, stations), jnp.int32),
            pltpu.SMEM((1, MAXP), jnp.int32),
            pltpu.VMEM((2, CHUNKS, HOP, CHUNK), jnp.bfloat16),
            pltpu.VMEM((NBIN, NBIN), jnp.bfloat16),
            pltpu.VMEM((2 * PAD + blocks, wide), jnp.float32),
            pltpu.VMEM((2, PAD, wide), jnp.float32),
            pltpu.VMEM((2 * stations, HOP), jnp.bfloat16),
            pltpu.VMEM((stations, 2 * NBIN), jnp.float32),
            pltpu.VMEM((stations, 2 * NBIN), jnp.float32),
            pltpu.VMEM((CHUNKS, near_rows, CHUNK), jnp.bfloat16),
            pltpu.VMEM((CHUNKS, stations - near_rows, CHUNK), jnp.bfloat16),
            pltpu.VMEM((CHUNKS, near_rows, CHUNK), jnp.bfloat16),
            pltpu.VMEM((CHUNKS, stations - near_rows, CHUNK), jnp.bfloat16),
            pltpu.VMEM((3, slabs, 2, SUB, bins), jnp.bfloat16),
            pltpu.VMEM((3, slabs, 2, SUB, bins), jnp.bfloat16),
            pltpu.VMEM(whole_shape, jnp.bfloat16),
            pltpu.VMEM(split_shape, jnp.bfloat16),
            pltpu.VMEM((groups,) + whole_shape, jnp.bfloat16),
            pltpu.VMEM((groups,) + split_shape, jnp.bfloat16),
            pltpu.VMEM((2 * slabs, bins, pairs), jnp.float32),
            pltpu.VMEM((MAXP, 2 * slabs, bins, pairs), jnp.float32),
            dma((4,)),
            dma((2, CHUNKS)),
            dma((2,)),
            dma((2,)),
            dma((2,)),
            dma((2 * CHUNKS,)),
            dma((2 * CHUNKS,)),
            dma((3 * (slabs - 1),)),
            dma((3 * (slabs - 1),)),
            dma((2 * (groups - 1),)),
            dma((2 * (groups - 1),)),
        ],
        compiler_params=pltpu.CompilerParams(
            collective_id=0, has_side_effects=True, vmem_limit_bytes=VMEM_BYTES
        ),
    )(raw_data, pltpu.with_memory_space_constraint(station_group[None, :], pltpu.HBM), pltpu.with_memory_space_constraint(partner_blocks, pltpu.HBM), dft_table())


def solution(mesh):
    placed = (P("stn", ("hour", "tchunk")), P("stn"), P("stn", None))
    return jax.shard_map(
        body,
        mesh=mesh,
        in_specs=placed,
        out_specs=P(("hour", "stn"), None, "tchunk", None),
        check_vma=False,
    )
```

```python
import functools
import math

import jax
import jax.numpy as jnp
import numpy as np
from jax import lax
from jax.experimental import pallas as pl
from jax.experimental.pallas import tpu as pltpu
from jax.sharding import PartitionSpec as P

SEGLEN = 4096
HOP = 2048
NBIN = 512
RB = 128
RAMH = 10
SMOOTH = 8
SUB = 16
MAXP = 3
PAD = 16
LANES = 128
CHUNK = 2 * LANES
CHUNKS = 2 * NBIN // CHUNK
VMEM_BYTES = 54000 * 1024

EPS_MEAN = 1e-06
LEVEL = 0.05
MESH = pl.DeviceIdType.MESH


def dft_table():
    sample = np.arange(SEGLEN)
    angles = (sample[:, None] * np.arange(1, NBIN + 1)[None, :] % SEGLEN) * (2.0 * math.pi / SEGLEN)
    taper = (0.5 - 0.5 * np.cos(sample * (2.0 * math.pi / SEGLEN)))[:, None]
    parts = np.stack([taper * np.cos(angles), -taper * np.sin(angles)])
    parts = parts.reshape(2, 2, HOP, CHUNKS, LANES).transpose(1, 3, 2, 0, 4)
    matrix = parts.reshape(2, CHUNKS, HOP, CHUNK)
    return jnp.asarray(matrix.astype(np.float32).astype(jnp.bfloat16))


def whiten(spectra, near):
    starts = range(0, 2 * NBIN, CHUNK)
    real_part = jnp.concatenate([spectra[:, at : at + LANES] for at in starts], axis=1)
    imag_part = jnp.concatenate([spectra[:, at + LANES : at + CHUNK] for at in starts], axis=1)
    powers = real_part * real_part + imag_part * imag_part
    bins = lax.broadcasted_iota(jnp.int32, (1, NBIN), 1)
    count = jnp.minimum(bins + SMOOTH, NBIN - 1) - jnp.maximum(bins - SMOOTH, 0) + 1
    high = powers.astype(jnp.bfloat16)
    rest = (powers - high.astype(jnp.float32)).astype(jnp.bfloat16)
    total = jnp.dot(high, near, preferred_element_type=jnp.float32) + jnp.dot(
        rest, near, preferred_element_type=jnp.float32
    )
    smooth = total * (1.0 / count.astype(jnp.float32))
    floor_level = jnp.sum(powers, axis=1, keepdims=True) * (1.0 / NBIN) + 1e-06
    scale = lax.rsqrt(smooth + LEVEL * floor_level)
    return jnp.concatenate([real_part * scale, imag_part * scale], axis=1).astype(jnp.bfloat16)


def spectra_kernel(
    slabs,
    groups,
    near_rows,
    raw_hbm,
    group_hbm,
    partner_hbm,
    table_hbm,
    out_ref,
    raw_ref,
    group_ref,
    partner_ref,
    table,
    nearby,
    sums,
    edge_out,
    halo,
    norm,
    own,
    keep,
    near_out,
    far_out,
    near_in,
    far_in,
    outbox,
    inbox,
    spread_whole,
    spread_split,
    gathered_whole,
    gathered_split,
    mine,
    other,
    raw_sem,
    table_sem,
    argument_sem,
    sum_send,
    sum_recv,
    hop_send,
    hop_recv,
    mix_send,
    mix_recv,
    all_send,
    all_recv,
):
    stations, samples = raw_ref.shape
    blocks = samples // RB
    bins = NBIN // slabs
    t = lax.axis_index("tchunk")
    b = lax.axis_index("stn")
    has_next = t < slabs - 1
    has_prev = t > 0
    nxt = jnp.minimum(t + 1, slabs - 1)
    prv = jnp.maximum(t - 1, 0)

    edge, middle = RAMH, blocks - RAMH
    spans = (range(edge), range(middle, blocks), range(edge, middle))
    loads = []
    for part, span in enumerate(spans):
        columns = slice(span[0] * RB, (span[-1] + 1) * RB)
        load = pltpu.make_async_copy(
            raw_hbm.at[:, columns], raw_ref.at[:, columns], raw_sem.at[part]
        )
        load.start()
        loads.append(load)
    fetches = [
        [
            pltpu.make_async_copy(
                table_hbm.at[side, part], table.at[side, part], table_sem.at[side, part]
            )
            for part in range(CHUNKS)
        ]
        for side in range(2)
    ]
    argument_loads = (
        pltpu.make_async_copy(group_hbm, group_ref, argument_sem.at[0]),
        pltpu.make_async_copy(partner_hbm, partner_ref, argument_sem.at[1]),
    )

    barrier = pltpu.get_barrier_semaphore()
    for step in range(1, slabs):
        pl.semaphore_signal(
            barrier, inc=1, device_id={"tchunk": lax.rem(t + step, slabs)}, device_id_type=MESH
        )
    for step in range(1, groups):
        pl.semaphore_signal(
            barrier, inc=1, device_id={"stn": lax.rem(b + step, groups)}, device_id_type=MESH
        )

    wide = sums.shape[1]
    lane = lax.broadcasted_iota(jnp.int32, (stations, LANES), 1)
    def add_sums(acc, span):
        for block in span:
            columns = slice(block * RB, (block + 1) * RB)
            part = jnp.sum(jnp.abs(raw_ref[:, columns]), axis=1, keepdims=True)
            acc = jnp.where(lane == block, part, acc)
        return acc

    def by_block(acc):
        tall = jnp.concatenate([acc, jnp.zeros((wide - stations, LANES), jnp.float32)], axis=0)
        return tall.T[:blocks, :]

    loads[0].wait()
    acc = add_sums(jnp.zeros((stations, LANES), jnp.float32), spans[0])
    for load in loads[1:]:
        load.wait()
    for copy in [*(fetches[at % 2][at // 2] for at in range(2 * CHUNKS)), *argument_loads]:
        copy.start()
    acc = add_sums(acc, spans[1])
    ends = by_block(acc)
    edge_out[0] = ends[blocks - PAD :]
    edge_out[1] = ends[:PAD]

    pl.semaphore_wait(barrier, slabs - 1 + groups - 1)

    def remote(source, target, sends, recvs, index, place):
        return pltpu.make_async_remote_copy(
            src_ref=source,
            dst_ref=target,
            send_sem=sends.at[index],
            recv_sem=recvs.at[index],
            device_id=place,
            device_id_type=MESH,
        )

    up = {"tchunk": nxt}
    down = {"tchunk": prv}
    sums_up = remote(edge_out.at[0], halo.at[0], sum_send, sum_recv, 0, up)
    sums_down = remote(edge_out.at[1], halo.at[1], sum_send, sum_recv, 1, down)

    @pl.when(has_next)
    def _():
        sums_up.start()

    @pl.when(has_prev)
    def _():
        sums_down.start()

    sums[0:PAD, :] = jnp.zeros((PAD, wide), jnp.float32)
    sums[PAD : PAD + blocks, :] = by_block(add_sums(acc, spans[2]))
    sums[PAD + blocks : 2 * PAD + blocks, :] = jnp.zeros((PAD, wide), jnp.float32)

    def inverses():
        window = sums[PAD - RAMH : PAD - RAMH + blocks, :]
        for offset in range(1, 2 * RAMH):
            window = window + sums[PAD - RAMH + offset : PAD - RAMH + offset + blocks, :]
        here = t * blocks + lax.broadcasted_iota(jnp.int32, (blocks, wide), 0)
        counted = jnp.minimum(here + RAMH, blocks * slabs) - jnp.maximum(here - RAMH, 0)
        running = window / (RB * counted.astype(jnp.float32))
        inverse = 1.0 / (running + EPS_MEAN)
        return jnp.concatenate(
            [inverse, jnp.zeros((LANES - blocks, wide), jnp.float32)], axis=0
        ).T[:stations, :]

    def normalize(inverse, chosen):
        for block in chosen:
            columns = slice(block * RB, (block + 1) * RB)
            rows = slice(block * RB // HOP * stations, (block * RB // HOP + 1) * stations)
            place = slice(block * RB % HOP, block * RB % HOP + RB)
            norm[rows, place] = (raw_ref[:, columns] * inverse[:, block : block + 1]).astype(
                jnp.bfloat16
            )

    first, last = RAMH, blocks - RAMH + 1
    normalize(inverses(), range(first, last))

    @pl.when(jnp.logical_not(has_prev))
    def _():
        far_in[...] = jnp.zeros_like(far_in)

    @pl.when(jnp.logical_not(has_next))
    def _():
        near_in[...] = jnp.zeros_like(near_in)

    @pl.when(has_prev)
    def _():
        sums_up.wait_recv()
        sums[0:PAD, :] = halo[0]

    @pl.when(has_next)
    def _():
        sums_down.wait_recv()
        sums[PAD + blocks : 2 * PAD + blocks, :] = halo[1]

    normalize(inverses(), [*range(first), *range(last, blocks)])

    row = lax.broadcasted_iota(jnp.int32, (NBIN, NBIN), 0)
    col = lax.broadcasted_iota(jnp.int32, (NBIN, NBIN), 1)
    nearby[...] = (jnp.abs(row - col) <= SMOOTH).astype(jnp.float32).astype(jnp.bfloat16)
    for load in argument_loads:
        load.wait()
    member = (
        group_ref[...] == lax.broadcasted_iota(jnp.int32, (SUB, stations), 0)
    ).astype(jnp.float32)

    def put_beams(pieces, spectra, members):
        sums_here = jnp.dot(
            members.astype(jnp.bfloat16),
            whiten(spectra, nearby[...]),
            preferred_element_type=jnp.float32,
        ).astype(jnp.bfloat16)
        for index, piece in enumerate(pieces):
            rows = slice(index * SUB, (index + 1) * SUB)
            for part in range(2):
                for slab in range(slabs):
                    begin = part * NBIN + slab * bins
                    outbox[piece, slab, part] = sums_here[rows, begin : begin + bins]
        copies = []
        for step in range(slabs - 1, 0, -1):
            to = lax.rem(t + step, slabs)
            for piece in pieces:
                copy = remote(
                    outbox.at[piece, to],
                    inbox.at[piece, t],
                    mix_send,
                    mix_recv,
                    piece * (slabs - 1) + step - 1,
                    {"tchunk": to},
                )
                copy.start()
                copies.append(copy)
        for piece in pieces:
            inbox[piece, t] = outbox[piece, t]
        return copies

    spreads = (spread_whole, spread_split)
    gathers = (gathered_whole, gathered_split)

    def share(half):
        copies = []
        for step in range(1, groups):
            copy = remote(
                spreads[half],
                gathers[half].at[b],
                all_send,
                all_recv,
                half * (groups - 1) + step - 1,
                {"stn": lax.rem(b + step, groups)},
            )
            copy.start()
            copies.append(copy)
        gathers[half][b] = spreads[half][...]
        return copies

    pairs = SUB * SUB
    pair_row = lax.broadcasted_iota(jnp.int32, (SUB, pairs), 0)
    pair_col = lax.broadcasted_iota(jnp.int32, (SUB, pairs), 1)
    left_hot = (pair_col // SUB == pair_row).astype(jnp.float32).astype(jnp.bfloat16)
    right_hot = (pair_col % SUB == pair_row).astype(jnp.float32).astype(jnp.bfloat16)

    def expand(beams, hot):
        return lax.dot_general(
            beams, hot, (((0,), (0,)), ((), ())), preferred_element_type=jnp.float32
        )

    def expand_mine(half):
        for index in range(spreads[half].shape[0]):
            mine[index] = expand(spreads[half][index], left_hot)

    def stack(half):
        count = spreads[half].shape[0]
        tile = 8
        for slot in range(MAXP):
            partner = partner_ref[0, slot]
            chosen = jnp.maximum(partner, 0)
            weight = jnp.where(partner >= 0, 1.0 / (2 * slabs - 1), 0.0)
            for index in range(count):
                other[slot, index] = expand(gathers[half][chosen, index], right_hot)

            for step in range(bins // tile):
                rows = slice(step * tile, (step + 1) * tile)
                if half == 0:
                    real_sum = jnp.zeros((tile, pairs), jnp.float32)
                    imag_sum = jnp.zeros((tile, pairs), jnp.float32)
                else:
                    real_sum = out_ref[0, slot, rows, 0:pairs]
                    imag_sum = out_ref[0, slot, rows, pairs : 2 * pairs]
                for segment in range(count // 2):
                    a = mine[2 * segment, rows]
                    c = mine[2 * segment + 1, rows]
                    d = other[slot, 2 * segment, rows]
                    e = other[slot, 2 * segment + 1, rows]
                    real_sum = real_sum + a * d + c * e
                    imag_sum = imag_sum + c * d - a * e
                if half == 1:
                    real_sum = real_sum * weight
                    imag_sum = imag_sum * weight
                out_ref[0, slot, rows, 0:pairs] = real_sum
                out_ref[0, slot, rows, pairs : 2 * pairs] = imag_sum

    def dot(left, right):
        return jnp.dot(left, right, preferred_element_type=jnp.float32)

    near_copies = []
    far_copies = []
    for part in range(CHUNKS):
        columns = slice(part * CHUNK, (part + 1) * CHUNK)
        fetches[0][part].wait()
        fetches[1][part].wait()
        opening = dot(norm[stations:], table[0, part])
        closing = dot(norm[:stations], table[1, part])
        far_out[part] = opening[near_rows:].astype(jnp.bfloat16)
        near_out[part] = closing[:near_rows].astype(jnp.bfloat16)
        keep[:near_rows, columns] = opening[:near_rows]
        keep[near_rows:, columns] = closing[near_rows:]
        far_copies.append(remote(far_out.at[part], far_in.at[part], hop_send, hop_recv, part, up))
        near_copies.append(
            remote(near_out.at[part], near_in.at[part], hop_send, hop_recv, CHUNKS + part, down)
        )
        pl.when(has_next)(far_copies[-1].start)
        pl.when(has_prev)(near_copies[-1].start)

    for part in range(CHUNKS):
        columns = slice(part * CHUNK, (part + 1) * CHUNK)
        own[:, columns] = dot(norm[:stations], table[0, part]) + dot(norm[stations:], table[1, part])
    mixes = put_beams((0,), own[...], member)

    @pl.when(has_next)
    def _():
        for copy in near_copies:
            copy.wait_recv()

    @pl.when(has_prev)
    def _():
        for copy in far_copies:
            copy.wait_recv()

    for part in range(CHUNKS):
        columns = slice(part * CHUNK, (part + 1) * CHUNK)
        own[:near_rows, columns] = keep[:near_rows, columns] + near_in[part].astype(jnp.float32)
        own[near_rows:, columns] = keep[near_rows:, columns] + far_in[part].astype(jnp.float32)
    station = lax.broadcasted_iota(jnp.int32, (SUB, stations), 1)
    split_member = jnp.concatenate(
        [jnp.where(station < near_rows, member, 0.0), jnp.where(station < near_rows, 0.0, member)],
        axis=0,
    )
    split_mixes = put_beams((1, 2), own[...], split_member)

    for copy in mixes:
        copy.wait()
    for slab in range(slabs):
        for part in range(2):
            spread_whole[2 * slab + part] = inbox[0, slab, part]
    whole_shares = share(0)
    expand_mine(0)

    for copy in split_mixes:
        copy.wait()
    for slab in range(slabs - 1):
        for part in range(2):
            both = inbox[1, slab, part].astype(jnp.float32)
            both = both + inbox[2, slab + 1, part].astype(jnp.float32)
            spread_split[2 * slab + part] = both.astype(jnp.bfloat16)
    split_shares = share(1)

    for copy in whole_shares:
        copy.wait()
    stack(0)
    expand_mine(1)

    @pl.when(has_next)
    def _():
        sums_up.wait_send()
        for copy in far_copies:
            copy.wait_send()

    @pl.when(has_prev)
    def _():
        sums_down.wait_send()
        for copy in near_copies:
            copy.wait_send()

    for copy in split_shares:
        copy.wait()
    stack(1)


def body(raw_data, station_group, partner_blocks):
    stations, samples = raw_data.shape
    slabs = lax.axis_size("tchunk")
    groups = lax.axis_size("stn")
    bins = NBIN // slabs
    blocks = samples // RB
    near_rows = -(-stations // 16) * 8
    wide = -(-stations // LANES) * LANES
    vmem = pl.BlockSpec(memory_space=pltpu.VMEM)
    dma = pltpu.SemaphoreType.DMA
    pairs = SUB * SUB
    whole_shape = (2 * slabs, SUB, bins)
    split_shape = (2 * slabs - 2, SUB, bins)
    far = pl.BlockSpec(memory_space=pltpu.HBM)
    return pl.pallas_call(
        functools.partial(spectra_kernel, slabs, groups, near_rows),
        out_shape=jax.ShapeDtypeStruct((1, MAXP, bins, 2 * pairs), jnp.float32),
        in_specs=[far, far, far, far],
        out_specs=vmem,
        scratch_shapes=[
            pltpu.VMEM((stations, samples), jnp.float32),
            pltpu.VMEM((1, stations), jnp.int32),
            pltpu.SMEM((1, MAXP), jnp.int32),
            pltpu.VMEM((2, CHUNKS, HOP, CHUNK), jnp.bfloat16),
            pltpu.VMEM((NBIN, NBIN), jnp.bfloat16),
            pltpu.VMEM((2 * PAD + blocks, wide), jnp.float32),
            pltpu.VMEM((2, PAD, wide), jnp.float32),
            pltpu.VMEM((2, PAD, wide), jnp.float32),
            pltpu.VMEM((2 * stations, HOP), jnp.bfloat16),
            pltpu.VMEM((stations, 2 * NBIN), jnp.float32),
            pltpu.VMEM((stations, 2 * NBIN), jnp.float32),
            pltpu.VMEM((CHUNKS, near_rows, CHUNK), jnp.bfloat16),
            pltpu.VMEM((CHUNKS, stations - near_rows, CHUNK), jnp.bfloat16),
            pltpu.VMEM((CHUNKS, near_rows, CHUNK), jnp.bfloat16),
            pltpu.VMEM((CHUNKS, stations - near_rows, CHUNK), jnp.bfloat16),
            pltpu.VMEM((3, slabs, 2, SUB, bins), jnp.bfloat16),
            pltpu.VMEM((3, slabs, 2, SUB, bins), jnp.bfloat16),
            pltpu.VMEM(whole_shape, jnp.bfloat16),
            pltpu.VMEM(split_shape, jnp.bfloat16),
            pltpu.VMEM((groups,) + whole_shape, jnp.bfloat16),
            pltpu.VMEM((groups,) + split_shape, jnp.bfloat16),
            pltpu.VMEM((2 * slabs, bins, pairs), jnp.float32),
            pltpu.VMEM((MAXP, 2 * slabs, bins, pairs), jnp.float32),
            dma((3,)),
            dma((2, CHUNKS)),
            dma((2,)),
            dma((2,)),
            dma((2,)),
            dma((2 * CHUNKS,)),
            dma((2 * CHUNKS,)),
            dma((3 * (slabs - 1),)),
            dma((3 * (slabs - 1),)),
            dma((2 * (groups - 1),)),
            dma((2 * (groups - 1),)),
        ],
        compiler_params=pltpu.CompilerParams(
            collective_id=0, has_side_effects=True, vmem_limit_bytes=VMEM_BYTES
        ),
    )(raw_data, pltpu.with_memory_space_constraint(station_group[None, :], pltpu.HBM), pltpu.with_memory_space_constraint(partner_blocks, pltpu.HBM), dft_table())


def solution(mesh):
    placed = (P("stn", ("hour", "tchunk")), P("stn"), P("stn", None))
    return jax.shard_map(
        body,
        mesh=mesh,
        in_specs=placed,
        out_specs=P(("hour", "stn"), None, "tchunk", None),
        check_vma=False,
    )
```

```python
import functools
import math

import jax
import jax.numpy as jnp
import numpy as np
from jax import lax
from jax.experimental import pallas as pl
from jax.experimental.pallas import tpu as pltpu
from jax.sharding import PartitionSpec as P

SEGLEN = 4096
HOP = 2048
NBIN = 512
RB = 128
RAMH = 10
SMOOTH = 8
SUB = 16
MAXP = 3
PAD = 16
LANES = 128
CHUNK = 2 * LANES
CHUNKS = 2 * NBIN // CHUNK
VMEM_BYTES = 54000 * 1024

EPS_MEAN = 1e-06
LEVEL = 0.05
MESH = pl.DeviceIdType.MESH


def dft_table():
    sample = np.arange(SEGLEN)
    angles = (sample[:, None] * np.arange(1, NBIN + 1)[None, :] % SEGLEN) * (2.0 * math.pi / SEGLEN)
    taper = (0.5 - 0.5 * np.cos(sample * (2.0 * math.pi / SEGLEN)))[:, None]
    parts = np.stack([taper * np.cos(angles), -taper * np.sin(angles)])
    parts = parts.reshape(2, 2, HOP, CHUNKS, LANES).transpose(1, 3, 2, 0, 4)
    matrix = parts.reshape(2, CHUNKS, HOP, CHUNK)
    return jnp.asarray(matrix.astype(np.float32).astype(jnp.bfloat16))


def whiten(spectra, near):
    starts = range(0, 2 * NBIN, CHUNK)
    real_part = jnp.concatenate([spectra[:, at : at + LANES] for at in starts], axis=1)
    imag_part = jnp.concatenate([spectra[:, at + LANES : at + CHUNK] for at in starts], axis=1)
    powers = real_part * real_part + imag_part * imag_part
    bins = lax.broadcasted_iota(jnp.int32, (1, NBIN), 1)
    count = jnp.minimum(bins + SMOOTH, NBIN - 1) - jnp.maximum(bins - SMOOTH, 0) + 1
    high = powers.astype(jnp.bfloat16)
    rest = (powers - high.astype(jnp.float32)).astype(jnp.bfloat16)
    total = jnp.dot(high, near, preferred_element_type=jnp.float32) + jnp.dot(
        rest, near, preferred_element_type=jnp.float32
    )
    smooth = total * (1.0 / count.astype(jnp.float32))
    floor_level = jnp.sum(powers, axis=1, keepdims=True) * (1.0 / NBIN) + 1e-06
    scale = lax.rsqrt(smooth + LEVEL * floor_level)
    return jnp.concatenate([real_part * scale, imag_part * scale], axis=1).astype(jnp.bfloat16)


def spectra_kernel(
    slabs,
    groups,
    near_rows,
    raw_hbm,
    group_hbm,
    partner_hbm,
    table_hbm,
    out_ref,
    raw_ref,
    group_ref,
    partner_ref,
    table,
    nearby,
    sums,
    edge_out,
    halo,
    norm,
    own,
    keep,
    near_out,
    far_out,
    near_in,
    far_in,
    outbox,
    inbox,
    spread_whole,
    spread_split,
    gathered_whole,
    gathered_split,
    mine,
    other,
    raw_sem,
    table_sem,
    argument_sem,
    sum_send,
    sum_recv,
    hop_send,
    hop_recv,
    mix_send,
    mix_recv,
    all_send,
    all_recv,
):
    stations, samples = raw_ref.shape
    blocks = samples // RB
    bins = NBIN // slabs
    t = lax.axis_index("tchunk")
    b = lax.axis_index("stn")
    has_next = t < slabs - 1
    has_prev = t > 0
    nxt = jnp.minimum(t + 1, slabs - 1)
    prv = jnp.maximum(t - 1, 0)

    edge, middle = RAMH, blocks - RAMH
    spans = (range(edge), range(middle, blocks), range(edge, middle))
    loads = []
    for part, span in enumerate(spans):
        columns = slice(span[0] * RB, (span[-1] + 1) * RB)
        load = pltpu.make_async_copy(
            raw_hbm.at[:, columns], raw_ref.at[:, columns], raw_sem.at[part]
        )
        load.start()
        loads.append(load)
    fetches = [
        [
            pltpu.make_async_copy(
                table_hbm.at[side, part], table.at[side, part], table_sem.at[side, part]
            )
            for part in range(CHUNKS)
        ]
        for side in range(2)
    ]
    argument_loads = (
        pltpu.make_async_copy(group_hbm, group_ref, argument_sem.at[0]),
        pltpu.make_async_copy(partner_hbm, partner_ref, argument_sem.at[1]),
    )

    barrier = pltpu.get_barrier_semaphore()
    for step in range(1, slabs):
        pl.semaphore_signal(
            barrier, inc=1, device_id={"tchunk": lax.rem(t + step, slabs)}, device_id_type=MESH
        )
    for step in range(1, groups):
        pl.semaphore_signal(
            barrier, inc=1, device_id={"stn": lax.rem(b + step, groups)}, device_id_type=MESH
        )

    wide = sums.shape[1]
    lane = lax.broadcasted_iota(jnp.int32, (stations, LANES), 1)
    def add_sums(acc, span):
        for block in span:
            columns = slice(block * RB, (block + 1) * RB)
            part = jnp.sum(jnp.abs(raw_ref[:, columns]), axis=1, keepdims=True)
            acc = jnp.where(lane == block, part, acc)
        return acc

    def by_block(acc):
        tall = jnp.concatenate([acc, jnp.zeros((wide - stations, LANES), jnp.float32)], axis=0)
        return tall.T[:blocks, :]

    loads[0].wait()
    acc = add_sums(jnp.zeros((stations, LANES), jnp.float32), spans[0])
    for load in loads[1:]:
        load.wait()
    for copy in [*argument_loads, *(fetches[at % 2][at // 2] for at in range(2 * CHUNKS))]:
        copy.start()
    acc = add_sums(acc, spans[1])
    ends = by_block(acc)
    edge_out[0] = ends[blocks - PAD :]
    edge_out[1] = ends[:PAD]

    pl.semaphore_wait(barrier, slabs - 1 + groups - 1)

    def remote(source, target, sends, recvs, index, place):
        return pltpu.make_async_remote_copy(
            src_ref=source,
            dst_ref=target,
            send_sem=sends.at[index],
            recv_sem=recvs.at[index],
            device_id=place,
            device_id_type=MESH,
        )

    up = {"tchunk": nxt}
    down = {"tchunk": prv}
    sums_up = remote(edge_out.at[0], halo.at[0], sum_send, sum_recv, 0, up)
    sums_down = remote(edge_out.at[1], halo.at[1], sum_send, sum_recv, 1, down)

    @pl.when(has_next)
    def _():
        sums_up.start()

    @pl.when(has_prev)
    def _():
        sums_down.start()

    sums[0:PAD, :] = jnp.zeros((PAD, wide), jnp.float32)
    sums[PAD : PAD + blocks, :] = by_block(add_sums(acc, spans[2]))
    sums[PAD + blocks : 2 * PAD + blocks, :] = jnp.zeros((PAD, wide), jnp.float32)

    def inverses():
        rows = blocks + 2 * RAMH - 2
        total = sums[PAD - RAMH : PAD - RAMH + rows, :] + sums[PAD - RAMH + 1 : PAD - RAMH + rows + 1, :]
        window = None
        count, begin = 2, 0
        while True:
            if 2 * RAMH & count:
                piece = total[begin : begin + blocks]
                window = piece if window is None else window + piece
                begin += count
            if 2 * count > 2 * RAMH:
                break
            total = total[: total.shape[0] - count] + total[count:]
            count *= 2
        here = t * blocks + lax.broadcasted_iota(jnp.int32, (blocks, wide), 0)
        counted = jnp.minimum(here + RAMH, blocks * slabs) - jnp.maximum(here - RAMH, 0)
        running = window / (RB * counted.astype(jnp.float32))
        inverse = 1.0 / (running + EPS_MEAN)
        return jnp.concatenate(
            [inverse, jnp.zeros((LANES - blocks, wide), jnp.float32)], axis=0
        ).T[:stations, :]

    def normalize(inverse, chosen):
        for block in chosen:
            columns = slice(block * RB, (block + 1) * RB)
            rows = slice(block * RB // HOP * stations, (block * RB // HOP + 1) * stations)
            place = slice(block * RB % HOP, block * RB % HOP + RB)
            norm[rows, place] = (raw_ref[:, columns] * inverse[:, block : block + 1]).astype(
                jnp.bfloat16
            )

    first, last = RAMH, blocks - RAMH + 1
    normalize(inverses(), range(first, last))

    @pl.when(jnp.logical_not(has_prev))
    def _():
        far_in[...] = jnp.zeros_like(far_in)

    @pl.when(jnp.logical_not(has_next))
    def _():
        near_in[...] = jnp.zeros_like(near_in)

    row = lax.broadcasted_iota(jnp.int32, (NBIN, NBIN), 0)
    col = lax.broadcasted_iota(jnp.int32, (NBIN, NBIN), 1)
    nearby[...] = (jnp.abs(row - col) <= SMOOTH).astype(jnp.float32).astype(jnp.bfloat16)
    for load in argument_loads:
        load.wait()
    member = (
        group_ref[...] == lax.broadcasted_iota(jnp.int32, (SUB, stations), 0)
    ).astype(jnp.float32)

    @pl.when(has_prev)
    def _():
        sums_up.wait_recv()
        sums[0:PAD, :] = halo[0]

    @pl.when(has_next)
    def _():
        sums_down.wait_recv()
        sums[PAD + blocks : 2 * PAD + blocks, :] = halo[1]

    normalize(inverses(), [*range(first), *range(last, blocks)])

    def put_beams(pieces, spectra, members):
        sums_here = jnp.dot(
            members.astype(jnp.bfloat16),
            whiten(spectra, nearby[...]),
            preferred_element_type=jnp.float32,
        ).astype(jnp.bfloat16)
        for index, piece in enumerate(pieces):
            rows = slice(index * SUB, (index + 1) * SUB)
            for part in range(2):
                for slab in range(slabs):
                    begin = part * NBIN + slab * bins
                    outbox[piece, slab, part] = sums_here[rows, begin : begin + bins]
        copies = []
        for step in range(slabs - 1, 0, -1):
            to = lax.rem(t + step, slabs)
            for piece in pieces:
                copy = remote(
                    outbox.at[piece, to],
                    inbox.at[piece, t],
                    mix_send,
                    mix_recv,
                    piece * (slabs - 1) + step - 1,
                    {"tchunk": to},
                )
                copy.start()
                copies.append(copy)
        for piece in pieces:
            inbox[piece, t] = outbox[piece, t]
        return copies

    spreads = (spread_whole, spread_split)
    gathers = (gathered_whole, gathered_split)

    def share(half):
        copies = []
        for step in range(1, groups):
            copy = remote(
                spreads[half],
                gathers[half].at[b],
                all_send,
                all_recv,
                half * (groups - 1) + step - 1,
                {"stn": lax.rem(b + step, groups)},
            )
            copy.start()
            copies.append(copy)
        gathers[half][b] = spreads[half][...]
        return copies

    pairs = SUB * SUB
    pair_row = lax.broadcasted_iota(jnp.int32, (SUB, pairs), 0)
    pair_col = lax.broadcasted_iota(jnp.int32, (SUB, pairs), 1)
    left_hot = (pair_col // SUB == pair_row).astype(jnp.float32).astype(jnp.bfloat16)
    right_hot = (pair_col % SUB == pair_row).astype(jnp.float32).astype(jnp.bfloat16)

    def expand(beams, hot):
        return lax.dot_general(
            beams, hot, (((0,), (0,)), ((), ())), preferred_element_type=jnp.float32
        )

    def expand_mine(half):
        for index in range(spreads[half].shape[0]):
            mine[index] = expand(spreads[half][index], left_hot)

    def stack(half):
        count = spreads[half].shape[0]
        tile = 8
        for slot in range(MAXP):
            partner = partner_ref[0, slot]
            chosen = jnp.maximum(partner, 0)
            weight = jnp.where(partner >= 0, 1.0 / (2 * slabs - 1), 0.0)
            for index in range(count):
                other[slot, index] = expand(gathers[half][chosen, index], right_hot)

            for step in range(bins // tile):
                rows = slice(step * tile, (step + 1) * tile)
                if half == 0:
                    real_sum = jnp.zeros((tile, pairs), jnp.float32)
                    imag_sum = jnp.zeros((tile, pairs), jnp.float32)
                else:
                    real_sum = out_ref[0, slot, rows, 0:pairs]
                    imag_sum = out_ref[0, slot, rows, pairs : 2 * pairs]
                for segment in range(count // 2):
                    a = mine[2 * segment, rows]
                    c = mine[2 * segment + 1, rows]
                    d = other[slot, 2 * segment, rows]
                    e = other[slot, 2 * segment + 1, rows]
                    real_sum = real_sum + a * d + c * e
                    imag_sum = imag_sum + c * d - a * e
                if half == 1:
                    real_sum = real_sum * weight
                    imag_sum = imag_sum * weight
                out_ref[0, slot, rows, 0:pairs] = real_sum
                out_ref[0, slot, rows, pairs : 2 * pairs] = imag_sum

    def dot(left, right):
        return jnp.dot(left, right, preferred_element_type=jnp.float32)

    near_copies = []
    far_copies = []
    for part in range(CHUNKS):
        columns = slice(part * CHUNK, (part + 1) * CHUNK)
        fetches[0][part].wait()
        fetches[1][part].wait()
        opening = dot(norm[stations:], table[0, part])
        closing = dot(norm[:stations], table[1, part])
        far_out[part] = opening[near_rows:].astype(jnp.bfloat16)
        near_out[part] = closing[:near_rows].astype(jnp.bfloat16)
        keep[:near_rows, columns] = opening[:near_rows]
        keep[near_rows:, columns] = closing[near_rows:]
        far_copies.append(remote(far_out.at[part], far_in.at[part], hop_send, hop_recv, part, up))
        near_copies.append(
            remote(near_out.at[part], near_in.at[part], hop_send, hop_recv, CHUNKS + part, down)
        )
        pl.when(has_next)(far_copies[-1].start)
        pl.when(has_prev)(near_copies[-1].start)

    for part in range(CHUNKS):
        columns = slice(part * CHUNK, (part + 1) * CHUNK)
        own[:, columns] = dot(norm[:stations], table[0, part]) + dot(norm[stations:], table[1, part])
    mixes = put_beams((0,), own[...], member)

    @pl.when(has_next)
    def _():
        for copy in near_copies:
            copy.wait_recv()

    @pl.when(has_prev)
    def _():
        for copy in far_copies:
            copy.wait_recv()

    for part in range(CHUNKS):
        columns = slice(part * CHUNK, (part + 1) * CHUNK)
        own[:near_rows, columns] = keep[:near_rows, columns] + near_in[part].astype(jnp.float32)
        own[near_rows:, columns] = keep[near_rows:, columns] + far_in[part].astype(jnp.float32)
    station = lax.broadcasted_iota(jnp.int32, (SUB, stations), 1)
    split_member = jnp.concatenate(
        [jnp.where(station < near_rows, member, 0.0), jnp.where(station < near_rows, 0.0, member)],
        axis=0,
    )
    split_mixes = put_beams((1, 2), own[...], split_member)

    for copy in mixes:
        copy.wait()
    for slab in range(slabs):
        for part in range(2):
            spread_whole[2 * slab + part] = inbox[0, slab, part]
    whole_shares = share(0)
    expand_mine(0)

    for copy in split_mixes:
        copy.wait()
    for slab in range(slabs - 1):
        for part in range(2):
            both = inbox[1, slab, part].astype(jnp.float32)
            both = both + inbox[2, slab + 1, part].astype(jnp.float32)
            spread_split[2 * slab + part] = both.astype(jnp.bfloat16)
    split_shares = share(1)

    for copy in whole_shares:
        copy.wait()
    stack(0)
    expand_mine(1)

    @pl.when(has_next)
    def _():
        sums_up.wait_send()
        for copy in far_copies:
            copy.wait_send()

    @pl.when(has_prev)
    def _():
        sums_down.wait_send()
        for copy in near_copies:
            copy.wait_send()

    for copy in split_shares:
        copy.wait()
    stack(1)


def body(raw_data, station_group, partner_blocks):
    stations, samples = raw_data.shape
    slabs = lax.axis_size("tchunk")
    groups = lax.axis_size("stn")
    bins = NBIN // slabs
    blocks = samples // RB
    near_rows = -(-stations // 16) * 8
    wide = -(-stations // LANES) * LANES
    vmem = pl.BlockSpec(memory_space=pltpu.VMEM)
    dma = pltpu.SemaphoreType.DMA
    pairs = SUB * SUB
    whole_shape = (2 * slabs, SUB, bins)
    split_shape = (2 * slabs - 2, SUB, bins)
    far = pl.BlockSpec(memory_space=pltpu.HBM)
    return pl.pallas_call(
        functools.partial(spectra_kernel, slabs, groups, near_rows),
        out_shape=jax.ShapeDtypeStruct((1, MAXP, bins, 2 * pairs), jnp.float32),
        in_specs=[far, far, far, far],
        out_specs=vmem,
        scratch_shapes=[
            pltpu.VMEM((stations, samples), jnp.float32),
            pltpu.VMEM((1, stations), jnp.int32),
            pltpu.SMEM((1, MAXP), jnp.int32),
            pltpu.VMEM((2, CHUNKS, HOP, CHUNK), jnp.bfloat16),
            pltpu.VMEM((NBIN, NBIN), jnp.bfloat16),
            pltpu.VMEM((2 * PAD + blocks, wide), jnp.float32),
            pltpu.VMEM((2, PAD, wide), jnp.float32),
            pltpu.VMEM((2, PAD, wide), jnp.float32),
            pltpu.VMEM((2 * stations, HOP), jnp.bfloat16),
            pltpu.VMEM((stations, 2 * NBIN), jnp.float32),
            pltpu.VMEM((stations, 2 * NBIN), jnp.float32),
            pltpu.VMEM((CHUNKS, near_rows, CHUNK), jnp.bfloat16),
            pltpu.VMEM((CHUNKS, stations - near_rows, CHUNK), jnp.bfloat16),
            pltpu.VMEM((CHUNKS, near_rows, CHUNK), jnp.bfloat16),
            pltpu.VMEM((CHUNKS, stations - near_rows, CHUNK), jnp.bfloat16),
            pltpu.VMEM((3, slabs, 2, SUB, bins), jnp.bfloat16),
            pltpu.VMEM((3, slabs, 2, SUB, bins), jnp.bfloat16),
            pltpu.VMEM(whole_shape, jnp.bfloat16),
            pltpu.VMEM(split_shape, jnp.bfloat16),
            pltpu.VMEM((groups,) + whole_shape, jnp.bfloat16),
            pltpu.VMEM((groups,) + split_shape, jnp.bfloat16),
            pltpu.VMEM((2 * slabs, bins, pairs), jnp.float32),
            pltpu.VMEM((MAXP, 2 * slabs, bins, pairs), jnp.float32),
            dma((3,)),
            dma((2, CHUNKS)),
            dma((2,)),
            dma((2,)),
            dma((2,)),
            dma((2 * CHUNKS,)),
            dma((2 * CHUNKS,)),
            dma((3 * (slabs - 1),)),
            dma((3 * (slabs - 1),)),
            dma((2 * (groups - 1),)),
            dma((2 * (groups - 1),)),
        ],
        compiler_params=pltpu.CompilerParams(
            collective_id=0, has_side_effects=True, vmem_limit_bytes=VMEM_BYTES
        ),
    )(raw_data, pltpu.with_memory_space_constraint(station_group[None, :], pltpu.HBM), pltpu.with_memory_space_constraint(partner_blocks, pltpu.HBM), dft_table())


def solution(mesh):
    placed = (P("stn", ("hour", "tchunk")), P("stn"), P("stn", None))
    return jax.shard_map(
        body,
        mesh=mesh,
        in_specs=placed,
        out_specs=P(("hour", "stn"), None, "tchunk", None),
        check_vma=False,
    )
```
